256 devices in a mesh: rep: 4 (over y), fsdp: 64 (over x, z, core).
Axes of the slice: x: 4, y: 4, z: 8, core: 2. Of those that a mesh axis runs over, the one named last changes fastest.
Arguments:
- grad_blocks: bfloat16 [4, 64, 512, 512], P('rep', None, 'fsdp'), may hold values from -6 to 6
- graft_accum: float32 [64, 512, 512], P(None, 'fsdp'), may hold values from 0.1 to 1000000
- left_stats: float32 [128, 512, 512], P('fsdp'), may hold values from -300000 to 300000, as said below
- right_stats: float32 [128, 512, 512], P('fsdp'), may hold values from -300000 to 300000, as said below
- block_slot: int32 [64], replicated, may hold values from 0 to 127, as said below
- vocab_grads: bfloat16 [4, 2, 512, 8192], P('rep', None, 'fsdp'), may hold values from -6 to 6
- vocab_accum: float32 [2, 512, 8192], P(None, 'fsdp'), may hold values from 0.01 to 10
Outputs:
- direction: bfloat16 [64, 512, 512], P(None, 'fsdp')
- graft_accum_new: float32 [64, 512, 512], P(None, 'fsdp')
- left_new: float32 [128, 512, 512], P('fsdp')
- right_new: float32 [128, 512, 512], P('fsdp')
- vocab_accum_new: float32 [2, 512, 8192], P(None, 'fsdp')
- vocab_step: bfloat16 [2, 512, 8192], P(None, 'fsdp')
The draws below stay inside these ranges and needn't reach their ends.
Inputs may be any that keep to these rules, and one draw needn't show every extreme that they name: Block b's statistics sit in slot block_slot[b]; slot s belongs to fsdp index s // 2; no two blocks name the same slot; every fsdp index owns at most 2 blocks and some index owns exactly 2. `left_stats`: every slot holds a symmetric positive definite matrix. `right_stats`: every slot holds a symmetric positive definite matrix.
All inputs are finite; a program needn't handle non-finite values.
Results may differ from the reference program's by a relative error of at most 0.017.
Values may be sent and summed in bfloat16 or wider, within the bound.
A program may use at most 64 MiB of HBM per device.

```python
import math
import jax
import jax.numpy as jnp
from jax import lax

D = 8192
B = 512
MOST = 2
ITERS = 6
NBLK = 64
SLOTS = 128
VOC = 512
N_REP = 4


def draw_block_slot(key, part):
    base = jax.random.fold_in(key, 11)
    first_key, second_key, third_key = jax.random.split(base, 3)
    workers = SLOTS // MOST
    full_worker = jax.random.randint(first_key, (), 0, workers)
    shuffled = jax.random.permutation(second_key, SLOTS).astype(jnp.int32)
    priority = (shuffled // MOST != full_worker).astype(jnp.int32) * SLOTS + jnp.arange(SLOTS, dtype=jnp.int32)
    ordered = shuffled[jnp.argsort(priority)]
    chosen = ordered[:NBLK]
    return chosen[jax.random.permutation(third_key, NBLK)].astype(jnp.int32)


def stats_draw(key, salt):
    base = jax.random.fold_in(key, salt)
    slot_keys = jax.random.split(base, SLOTS)
    order = float(B)

    def single(slot_key):
        first_key = jax.random.fold_in(slot_key, 0)
        second_key = jax.random.fold_in(slot_key, 1)
        fourth_key = jax.random.fold_in(slot_key, 3)
        fifth_key = jax.random.fold_in(slot_key, 4)
        factors = jax.random.normal(first_key, (B, 2 * B), jnp.float32)
        gram = jnp.dot(factors, factors.T, precision=lax.Precision.HIGHEST) / (2.0 * order)
        gram = 0.5 * (gram + gram.T)
        wishart_weight = 4.0 * order * jnp.exp(jax.random.uniform(second_key, (), jnp.float32, 0.0, jnp.log(3.0)))
        power = 1.0
        ranks = jax.random.permutation(fourth_key, B).astype(jnp.float32) + 1.0
        top_level = 8.0 * order * math.sqrt(order) * jnp.exp(jax.random.uniform(fifth_key, (), jnp.float32, 0.0, jnp.log(2.0)))
        spikes = top_level * jnp.power(ranks, -power)
        return wishart_weight * gram + jnp.diag(spikes)
    return lax.map(single, slot_keys)


def draw_left_stats(key, part):
    return stats_draw(key, 31)


def draw_right_stats(key, part):
    return stats_draw(key, 37)


def draw_graft_accum(key, part):
    base = jax.random.fold_in(key, 23)
    first_key, second_key, third_key = jax.random.split(base, 3)
    position = (jnp.arange(B, dtype=jnp.float32) / B)[None, :, None]
    jitter = jax.random.uniform(first_key, (NBLK, B, 1), jnp.float32)
    row_power = 2.0 * position + jitter
    column_power = 2.0 * jax.random.uniform(second_key, (NBLK, 1, B), jnp.float32)
    roughness = jax.random.uniform(third_key, (NBLK, B, B), jnp.float32, -0.7, 0.7)
    return jnp.power(10.0, row_power + column_power) * jnp.exp(roughness)


def block_scale(key, extent, cuts, low, high):
    loudness = 1.0
    for dim, blocks in cuts:
        steps = jax.random.uniform(jax.random.fold_in(jax.random.fold_in(key, 6), dim), (blocks,), jnp.float32, low / len(cuts), high / len(cuts))
        loudness = loudness * jnp.repeat(jnp.exp(steps), extent[dim] // blocks).reshape((-1,) + (1,) * (len(extent) - 1 - dim))
    return loudness


def gaussian(rng, shape, scale, limit, cuts=(), kind=jnp.bfloat16):
    loudness = block_scale(rng, shape, cuts, -0.22, 0.18) if cuts else 1.0
    array = jax.random.normal(rng, shape, jnp.float32) * scale * loudness
    return jnp.minimum(jnp.maximum(array, -limit), limit).astype(kind)


def setup_inputs(seed: int = 0) -> dict:
    key_list = jax.random.split(jax.random.key(seed), 8)
    grad_blocks = gaussian(key_list[0], (N_REP, NBLK, B, B), 1.0, 6.0, ((0, 4), (2, 64)))
    graft_accum = draw_graft_accum(jax.random.fold_in(key_list[7], 71), 0)
    left_stats = draw_left_stats(jax.random.fold_in(key_list[7], 71), 0)
    right_stats = draw_right_stats(jax.random.fold_in(key_list[7], 71), 0)
    block_slot = draw_block_slot(jax.random.fold_in(key_list[7], 71), 0)
    vocab_grads = gaussian(key_list[5], (N_REP, 2, VOC, D), 1.0, 6.0, ((0, 4), (2, 64)))
    vocab_accum = jnp.clip(jnp.exp(math.log(10.0) - 6.9077553 * jax.random.uniform(key_list[6], (2, VOC, D), jnp.float32) ** block_scale(key_list[6], (2, VOC, D), ((1, 64),), -0.2, 0.2)), 0.01, 10.0)
    return {"grad_blocks": grad_blocks, "graft_accum": graft_accum, "left_stats": left_stats, "right_stats": right_stats, "block_slot": block_slot, "vocab_grads": vocab_grads, "vocab_accum": vocab_accum}


def product(left, right):
    return jnp.dot(left, right, precision=lax.Precision.HIGHEST)

def inverse_root(matrix):
    identity = jnp.eye(matrix.shape[0], dtype=matrix.dtype)
    frobenius = jnp.sqrt(jnp.sum(matrix * matrix))
    scaled = matrix / frobenius
    result = identity
    for iteration in range(ITERS):
        factor = (5.0 * identity - scaled) * 0.25
        result = factor if iteration == 0 else product(result, factor)
        if iteration + 1 < ITERS:
            square = product(factor, factor)
            fourth = product(square, square)
            scaled = product(fourth, scaled)
    return result

def reference(grad_blocks, graft_accum, left_stats, right_stats, block_slot, vocab_grads, vocab_accum):
    grad_sum = lax.optimization_barrier(jnp.sum(grad_blocks.astype(jnp.float32), axis=0)).astype(jnp.bfloat16)
    vocab_sum = lax.optimization_barrier(jnp.sum(vocab_grads.astype(jnp.float32), axis=0)).astype(jnp.bfloat16)
    vocab_float = vocab_sum.astype(jnp.float32)
    vocab_accum_new = vocab_accum + vocab_float * vocab_float
    vocab_step = (vocab_float / (jnp.sqrt(vocab_accum_new) + 1e-10)).astype(jnp.bfloat16)
    grad_float = grad_sum.astype(jnp.float32)
    graft_accum_new = graft_accum + grad_float * grad_float
    grafted = grad_float / (jnp.sqrt(graft_accum_new) + 1e-10)
    graft_mean = lax.optimization_barrier(jnp.mean(grafted * grafted, axis=(1, 2)))

    def one_block(inputs):
        block_grad, slot_index, block_mean = inputs
        left_block = left_stats[slot_index] + jnp.dot(block_grad, block_grad.T, preferred_element_type=jnp.float32)
        right_block = right_stats[slot_index] + jnp.dot(block_grad.T, block_grad, preferred_element_type=jnp.float32)
        block_float = block_grad.astype(jnp.float32)
        shampoo = product(product(inverse_root(left_block), block_float), inverse_root(right_block))
        graft_scale = jnp.sqrt(block_mean) / jnp.sqrt(jnp.mean(shampoo * shampoo) + 1e-06)
        return ((shampoo * graft_scale).astype(jnp.bfloat16), left_block, right_block)
    direction, left_blocks, right_blocks = lax.map(one_block, (grad_sum, block_slot.astype(jnp.int32), graft_mean))
    left_new = left_stats.at[block_slot].set(left_blocks)
    right_new = right_stats.at[block_slot].set(right_blocks)
    return (direction, graft_accum_new, left_new, right_new, vocab_accum_new, vocab_step)
```

```python
import functools

import jax
import jax.numpy as jnp
from jax import lax
from jax.experimental import pallas as pl
from jax.experimental.pallas import tpu as pltpu
from jax.sharding import PartitionSpec as P

ITERS = 6
REP = 4
MESH = pl.DeviceIdType.MESH
F32 = jnp.float32
BF16 = jnp.bfloat16
ANY = pl.BlockSpec(memory_space=pl.ANY)
VMEM = pl.BlockSpec(memory_space=pltpu.VMEM)
SMEM = pl.BlockSpec(memory_space=pltpu.SMEM)


def remote(src, dst, send_sem, recv_sem, device):
    return pltpu.make_async_remote_copy(
        src_ref=src,
        dst_ref=dst,
        send_sem=send_sem,
        recv_sem=recv_sem,
        device_id=device,
        device_id_type=MESH,
    )


def enter(rep, own, shards):
    barrier = pltpu.get_barrier_semaphore()

    @pl.loop(1, shards)
    def _(step):
        other = lax.rem(own + step, shards)
        pl.semaphore_signal(barrier, inc=1, device_id=(rep, other), device_id_type=MESH)

    for step in range(1, REP):
        other = lax.rem(rep + step, REP)
        pl.semaphore_signal(barrier, inc=1, device_id=(other, own), device_id_type=MESH)
    return lambda: pl.semaphore_wait(barrier, shards - 1 + REP - 1)


class RingGather:
    def __init__(self, out, rep, own, send_sems, recv_sems):
        self.out, self.send_sems, self.recv_sems = out, send_sems, recv_sems
        right, left = lax.rem(rep + 1, REP), lax.rem(rep + REP - 1, REP)
        far = lax.rem(rep + 2, REP)
        half = out.shape[1] // 2
        first, second = pl.ds(0, half), pl.ds(half, half)
        to_right, to_left = (right, own), (left, own)
        self.sends = (
            self.copy(out.at[rep], 0, to_right),
            self.copy(out.at[rep], 1, to_left),
            self.copy(out.at[left, first], 2, to_right),
            self.copy(out.at[right, second], 3, to_left),
        )
        self.arrivals = (
            self.copy(out.at[left], 0, to_right),
            self.copy(out.at[right], 1, to_left),
            self.copy(out.at[far, first], 2, to_right),
            self.copy(out.at[far, second], 3, to_left),
        )

    def copy(self, piece, index, device):
        return remote(piece, piece, self.send_sems.at[index], self.recv_sems.at[index], device)

    def start(self):
        self.sends[0].start()
        self.sends[1].start()

    def forward(self):
        self.arrivals[0].wait_recv()
        self.sends[2].start()
        self.arrivals[1].wait_recv()
        self.sends[3].start()

    def finish(self):
        self.arrivals[2].wait_recv()
        self.arrivals[3].wait_recv()
        for send in self.sends:
            send.wait_send()


def exchange(shards, rep, own, source, target, send_sems, recv_sems):
    @pl.loop(1, shards)
    def _(step):
        other = lax.rem(own + step, shards)
        remote(source(other), target(own), send_sems.at[other], recv_sems.at[own], (rep, other)).start()

    def finish():
        @pl.loop(1, shards)
        def _(step):
            other = lax.rem(own + step, shards)
            remote(
                source(other), target(other), send_sems.at[other], recv_sems.at[other], (rep, other)
            ).wait_recv()

        @pl.loop(1, shards)
        def _(step):
            other = lax.rem(own + step, shards)
            remote(
                source(other), target(own), send_sems.at[other], recv_sems.at[own], (rep, other)
            ).wait_send()

    return finish


def gather_kernel(
    shards,
    key_ref,
    grad_ref,
    accum_ref,
    vocab_ref,
    slots_out,
    grad_out,
    vocab_out,
    graft_out,
    grad_own,
    grad_terms,
    grad_sum,
    accum_own,
    vocab_own,
    vocab_terms,
    vocab_sum,
    placement,
    outgoing,
    graft_part,
    graft_parts,
    graft_total,
    local_sems,
    term_sends,
    term_recvs,
    slot_sends,
    slot_recvs,
    part_sends,
    part_recvs,
    ring_sends,
    ring_recvs,
):
    rep, own = lax.axis_index("rep"), lax.axis_index("fsdp")
    blocks, rows, quarter = grad_own.shape
    vocab_quarter = vocab_own.shape[-1]

    def grad_columns(index):
        return pl.ds(pl.multiple_of(index * quarter, 128), quarter)

    def vocab_columns(index):
        return pl.ds(pl.multiple_of(index * vocab_quarter, 128), vocab_quarter)

    loads = (
        pltpu.make_async_copy(grad_ref.at[:, :, grad_columns(rep)], grad_own, local_sems.at[0]),
        pltpu.make_async_copy(accum_ref.at[:, :, grad_columns(rep)], accum_own, local_sems.at[1]),
        pltpu.make_async_copy(vocab_ref.at[:, :, vocab_columns(rep)], vocab_own, local_sems.at[2]),
    )
    for load in loads:
        load.start()
    entered = enter(rep, own, shards)

    total_rows = blocks * rows
    key = jnp.broadcast_to(key_ref[...], (shards * rows, total_rows))
    row = lax.broadcasted_iota(jnp.int32, (shards * rows, total_rows), 0)
    place = (row // rows) * (2 * rows) + lax.rem(row, rows)
    for slot in range(2):
        placement[slot] = jnp.where(key == place + slot * rows, 1.0, 0.0).astype(BF16)

    entered()
    grad_copies, vocab_copies = [], []
    for step in range(1, REP):
        other = lax.rem(rep + step, REP)
        grad_copies.append(
            remote(
                grad_ref.at[:, :, grad_columns(other)],
                grad_terms.at[step - 1],
                term_sends.at[step - 1],
                term_recvs.at[step - 1],
                (other, own),
            )
        )
        vocab_copies.append(
            remote(
                vocab_ref.at[:, :, vocab_columns(other)],
                vocab_terms.at[step - 1],
                term_sends.at[REP + step - 2],
                term_recvs.at[REP + step - 2],
                (other, own),
            )
        )
    for copy in grad_copies:
        copy.start()
    loads[0].wait()
    for copy in grad_copies:
        copy.wait_recv()
    total = grad_own[...].astype(F32)
    for step in range(REP - 1):
        total = total + grad_terms[step].astype(F32)
    rounded = total.astype(BF16)
    grad_sum[...] = rounded
    flat = total.reshape(total_rows, quarter).astype(BF16)
    for slot in range(2):
        placed = jnp.dot(placement[slot], flat, preferred_element_type=F32)
        outgoing[:, :, slot * quarter : (slot + 1) * quarter] = placed.reshape(
            shards, rows, quarter
        ).astype(BF16)
    slots_done = exchange(
        shards,
        rep,
        own,
        lambda other: outgoing.at[other],
        lambda source: slots_out.at[rep, source],
        slot_sends,
        slot_recvs,
    )
    keep = pltpu.make_async_copy(outgoing.at[own], slots_out.at[rep, own], local_sems.at[3])
    keep.start()
    for copy in vocab_copies:
        copy.start()
    keep_sum = pltpu.make_async_copy(grad_sum, grad_out.at[rep], local_sems.at[4])
    keep_sum.start()
    keep_sum.wait()
    grad_ring = RingGather(grad_out, rep, own, ring_sends.at[0], ring_recvs.at[0])
    grad_ring.start()

    loads[1].wait()
    value = flat.astype(F32)
    accum_new = accum_own[...].reshape(total_rows, quarter) + value * value
    grafted = value / (jnp.sqrt(accum_new) + 1e-10)
    slot_count = 2 * shards
    slot = lax.broadcasted_iota(jnp.int32, (slot_count, total_rows), 0)
    mine = jnp.where(jnp.broadcast_to(key_ref[...] // rows, (slot_count, total_rows)) == slot, 1.0, 0.0)
    by_slot = jnp.dot(mine, grafted * grafted, precision=lax.Precision.HIGHEST)
    ones = jnp.ones((8, quarter), F32)
    parts = lax.dot_general(
        ones, by_slot, (((1,), (1,)), ((), ())), precision=lax.Precision.HIGHEST
    )
    graft_part[...] = parts[:1]
    graft_parts[pl.ds(own, 1)] = parts[:1][None]
    parts_done = exchange(
        shards,
        rep,
        own,
        lambda other: graft_part,
        lambda source: graft_parts.at[source],
        part_sends,
        part_recvs,
    )

    loads[2].wait()
    for copy in vocab_copies:
        copy.wait_recv()
    vocab_total = vocab_own[...].astype(F32)
    for step in range(REP - 1):
        vocab_total = vocab_total + vocab_terms[step].astype(F32)
    vocab_sum[...] = vocab_total.astype(BF16)
    keep_vocab = pltpu.make_async_copy(vocab_sum, vocab_out.at[rep], local_sems.at[5])
    keep_vocab.start()
    keep_vocab.wait()
    vocab_ring = RingGather(vocab_out, rep, own, ring_sends.at[1], ring_recvs.at[1])
    vocab_ring.start()
    grad_ring.forward()

    keep.wait()
    slots_done()
    slot_ring = RingGather(slots_out, rep, own, ring_sends.at[2], ring_recvs.at[2])
    slot_ring.start()
    vocab_ring.forward()

    parts_done()
    graft_total[...] = jnp.sum(graft_parts[...], axis=0)
    keep_total = pltpu.make_async_copy(graft_total, graft_out.at[rep], local_sems.at[6])
    keep_total.start()
    total_copies = []
    for step in range(1, REP):
        other = lax.rem(rep + step, REP)
        index = 2 * (REP - 1) + step - 1
        copy = remote(
            graft_total, graft_out.at[rep], term_sends.at[index], term_recvs.at[index], (other, own)
        )
        copy.start()
        source = lax.rem(rep + REP - step, REP)
        arrival = remote(
            graft_total, graft_out.at[source], term_sends.at[index], term_recvs.at[index], (other, own)
        )
        total_copies.append((copy, arrival))

    slot_ring.forward()
    grad_ring.finish()
    vocab_ring.finish()
    slot_ring.finish()
    keep_total.wait()
    for copy, arrival in total_copies:
        arrival.wait_recv()
        copy.wait_send()
    for copy in grad_copies + vocab_copies:
        copy.wait_send()


def gather_grads(key, grads, accum, vocab):
    shards = lax.axis_size("fsdp")
    blocks, rows, order = grads.shape
    quarter = order // REP
    vocab_quarter = vocab.shape[-1] // REP
    vocab_shape = vocab.shape[:2] + (vocab_quarter,)
    dma = pltpu.SemaphoreType.DMA
    return pl.pallas_call(
        functools.partial(gather_kernel, shards),
        out_shape=(
            jax.ShapeDtypeStruct((REP, shards, rows, 2 * quarter), BF16),
            jax.ShapeDtypeStruct((REP, blocks, rows, quarter), BF16),
            jax.ShapeDtypeStruct((REP,) + vocab_shape, BF16),
            jax.ShapeDtypeStruct((REP, 1, 2 * shards), F32),
        ),
        in_specs=[VMEM, ANY, ANY, ANY],
        out_specs=(ANY, ANY, ANY, ANY),
        scratch_shapes=[
            pltpu.VMEM((blocks, rows, quarter), BF16),
            pltpu.VMEM((REP - 1, blocks, rows, quarter), BF16),
            pltpu.VMEM((blocks, rows, quarter), BF16),
            pltpu.VMEM((blocks, rows, quarter), F32),
            pltpu.VMEM(vocab_shape, BF16),
            pltpu.VMEM((REP - 1,) + vocab_shape, BF16),
            pltpu.VMEM(vocab_shape, BF16),
            pltpu.VMEM((2, shards * rows, blocks * rows), BF16),
            pltpu.VMEM((shards, rows, 2 * quarter), BF16),
            pltpu.VMEM((1, 2 * shards), F32),
            pltpu.VMEM((shards, 1, 2 * shards), F32),
            pltpu.VMEM((1, 2 * shards), F32),
            dma((7,)),
            dma((3 * (REP - 1),)),
            dma((3 * (REP - 1),)),
            dma((shards,)),
            dma((shards,)),
            dma((shards,)),
            dma((shards,)),
            dma((3, 4)),
            dma((3, 4)),
        ],
        compiler_params=pltpu.CompilerParams(collective_id=0, has_side_effects=True),
        name="gather_grads",
    )(key, grads, accum, vocab)


def return_kernel(shards, mine_ref, out, local_sem, sends, recvs, ring_sends, ring_recvs):
    rep, own = lax.axis_index("rep"), lax.axis_index("fsdp")
    enter(rep, own, shards)()
    done = exchange(
        shards,
        rep,
        own,
        lambda other: mine_ref.at[other],
        lambda source: out.at[rep, source],
        sends,
        recvs,
    )
    keep = pltpu.make_async_copy(mine_ref.at[own], out.at[rep, own], local_sem)
    keep.start()
    keep.wait()
    done()
    ring = RingGather(out, rep, own, ring_sends, ring_recvs)
    ring.start()
    ring.forward()
    ring.finish()


def return_rows(mine):
    shards = lax.axis_size("fsdp")
    dma = pltpu.SemaphoreType.DMA
    return pl.pallas_call(
        functools.partial(return_kernel, shards),
        out_shape=jax.ShapeDtypeStruct((REP,) + mine.shape, BF16),
        in_specs=[ANY],
        out_specs=ANY,
        scratch_shapes=[dma, dma((shards,)), dma((shards,)), dma((4,)), dma((4,))],
        compiler_params=pltpu.CompilerParams(collective_id=1, has_side_effects=True),
        name="return_rows",
    )(mine)


def product(left, right):
    return jnp.dot(left.astype(BF16), right.astype(BF16), preferred_element_type=F32)


def precondition_kernel(
    where_ref,
    slots_ref,
    graft_ref,
    left_ref,
    right_ref,
    mine_out,
    left_out,
    right_out,
    stats,
    scaled,
    result,
    load_sems,
    store_sems,
):
    rep, own = where_ref[0], where_ref[1]
    pick, half = rep // 2, lax.rem(rep, 2)
    order = stats.shape[-1]
    quarter = order // REP
    loads = []
    for turn in range(2):
        slot = pick if turn == 0 else 1 - pick
        for side, ref in enumerate((left_ref, right_ref)):
            loads.append(pltpu.make_async_copy(ref.at[slot], stats.at[turn, side], load_sems.at[turn, side]))
    for load in loads:
        load.start()

    def gradient(slot):
        columns = pl.ds(pl.multiple_of(slot * quarter, 128), quarter)
        return jnp.concatenate(
            [
                slots_ref[index, :, :, columns].astype(F32).reshape(order, quarter).astype(BF16)
                for index in range(REP)
            ],
            axis=1,
        )

    stores = []

    def update(turn):
        slot = pick if turn == 0 else 1 - pick
        grad = gradient(slot)
        for side, out in enumerate((left_out, right_out)):
            axis = 1 - side
            outer = lax.dot_general(grad, grad, (((axis,), (axis,)), ((), ())), preferred_element_type=F32)
            loads[2 * turn + side].wait()
            stats[turn, side] = stats[turn, side] + outer
            store = pltpu.make_async_copy(stats.at[turn, side], out.at[slot], store_sems.at[turn, side])
            store.start()
            stores.append(store)
        return grad

    grad = update(0)
    row = lax.broadcasted_iota(jnp.int32, (order, order), 0)
    column = lax.broadcasted_iota(jnp.int32, (order, order), 1)
    for side in range(2):
        matrix = stats[0, side]
        start = matrix / jnp.sqrt(jnp.sum(matrix * matrix))
        scaled[side] = start
        result[side] = jnp.where(row == column, 1.25, 0.0) - 0.25 * start

    @pl.loop(1, ITERS)
    def _(iteration):
        for side in range(2):
            value = scaled[side]
            excess = product(value, value) * 0.0625 - 0.625 * value
            change = product(excess, excess) + 3.125 * excess
            value = product(change, value) + 2.44140625 * value
            scaled[side] = value
            root = result[side]
            result[side] = 1.25 * root - 0.25 * product(root, value)

    shampoo = product(product(result[0], grad), result[1])
    entries = float(order * order)
    lane = lax.broadcasted_iota(jnp.int32, (1, graft_ref.shape[-1]), 1)
    graft_total = jnp.sum(jnp.where(lane == 2 * own + pick, jnp.sum(graft_ref[...], axis=0), 0.0))
    graft_mean = jnp.full((1, 1), graft_total / entries, F32)
    shampoo_mean = jnp.full((1, 1), jnp.sum(shampoo * shampoo) / entries, F32)
    scale = jnp.sqrt(graft_mean) / jnp.sqrt(shampoo_mean + 1e-06)
    direction = shampoo * scale
    direction = jnp.where(half == 0, direction[:, : order // 2], direction[:, order // 2 :])
    mine_out[...] = direction.reshape(mine_out.shape).astype(BF16)
    update(1)
    for store in stores:
        store.wait()


def precondition(where, slots, graft, left, right):
    rows = slots.shape[2]
    order = left.shape[-1]
    dma = pltpu.SemaphoreType.DMA
    return pl.pallas_call(
        precondition_kernel,
        out_shape=(
            jax.ShapeDtypeStruct((order // rows, rows, order // 2), BF16),
            jax.ShapeDtypeStruct(left.shape, F32),
            jax.ShapeDtypeStruct(right.shape, F32),
        ),
        in_specs=[SMEM, VMEM, VMEM, ANY, ANY],
        out_specs=(VMEM, ANY, ANY),
        scratch_shapes=[
            pltpu.VMEM((2, 2, order, order), F32),
            pltpu.VMEM((2, order, order), F32),
            pltpu.VMEM((2, order, order), F32),
            dma((2, 2)),
            dma((2, 2)),
        ],
        name="precondition",
    )(where, slots, graft, left, right)


def accumulate_kernel(grad_ref, accum_ref, vocab_ref, vocab_accum_ref, accum_out, vocab_out, step_out):
    grad = grad_ref[0].astype(F32)
    accum_out[...] = accum_ref[...] + grad * grad
    vocab = vocab_ref[0].astype(F32)
    vocab_accum = vocab_accum_ref[...] + vocab * vocab
    vocab_out[...] = vocab_accum
    step_out[...] = (vocab / (jnp.sqrt(vocab_accum) + 1e-10)).astype(BF16)


def accumulate(grads, accum, vocab, vocab_accum):
    def piece(array):
        return pl.BlockSpec((1,) + array.shape[1:], lambda index: (index, 0, 0, 0))

    def columns(array):
        return pl.BlockSpec(
            array.shape[:2] + (array.shape[2] // REP,), lambda index: (0, 0, index)
        )

    return pl.pallas_call(
        accumulate_kernel,
        grid=(REP,),
        out_shape=(
            jax.ShapeDtypeStruct(accum.shape, F32),
            jax.ShapeDtypeStruct(vocab_accum.shape, F32),
            jax.ShapeDtypeStruct(vocab_accum.shape, BF16),
        ),
        in_specs=[piece(grads), columns(accum), piece(vocab), columns(vocab_accum)],
        out_specs=(columns(accum), columns(vocab_accum), columns(vocab_accum)),
        name="accumulate",
    )(grads, accum, vocab, vocab_accum)


def select_kernel(slot_ref, rows_ref, out):
    half = rows_ref.shape[-1]

    @pl.loop(0, out.shape[0])
    def _(block):
        slot = slot_ref[block]
        owner, pick = slot // 2, lax.rem(slot, 2)
        for side in range(2):
            out[block, :, side * half : (side + 1) * half] = rows_ref[2 * pick + side, owner]


def select_rows(block_slot, rows):
    return pl.pallas_call(
        select_kernel,
        out_shape=jax.ShapeDtypeStruct(
            (block_slot.shape[0], rows.shape[2], 2 * rows.shape[3]), BF16
        ),
        in_specs=[SMEM, VMEM],
        out_specs=VMEM,
        name="select_rows",
    )(block_slot, rows)


def on_device(
    grad_blocks, graft_accum, left_stats, right_stats, block_slot, vocab_grads, vocab_accum
):
    rows = grad_blocks.shape[2]
    key = (block_slot[:, None] * rows + jnp.arange(rows, dtype=jnp.int32)[None]).reshape(1, -1)
    where = jnp.stack([lax.axis_index("rep"), lax.axis_index("fsdp")]).astype(jnp.int32)
    slots, grads, vocab, graft = gather_grads(key, grad_blocks[0], graft_accum, vocab_grads[0])
    mine, left_new, right_new = precondition(where, slots, graft, left_stats, right_stats)
    returned = return_rows(mine)
    accum_new, vocab_accum_new, vocab_step = accumulate(grads, graft_accum, vocab, vocab_accum)
    direction = select_rows(block_slot, returned)
    return (direction, accum_new, left_new, right_new, vocab_accum_new, vocab_step)


def solution(mesh):
    in_specs = (
        P("rep", None, "fsdp", None),
        P(None, "fsdp", None),
        P("fsdp", None, None),
        P("fsdp", None, None),
        P(),
        P("rep", None, "fsdp", None),
        P(None, "fsdp", None),
    )
    out_specs = (
        P(None, "fsdp", None),
        P(None, "fsdp", None),
        P("fsdp", None, None),
        P("fsdp", None, None),
        P(None, "fsdp", None),
        P(None, "fsdp", None),
    )
    return jax.shard_map(
        on_device, mesh=mesh, in_specs=in_specs, out_specs=out_specs, check_vma=False
    )
```

```python
import functools

import jax
import jax.numpy as jnp
from jax import lax
from jax.experimental import pallas as pl
from jax.experimental.pallas import tpu as pltpu
from jax.sharding import PartitionSpec as P

ITERS = 6
REP = 4
GROUPS = 4
TURNS = (2, 1, 3, 0)
MESH = pl.DeviceIdType.MESH
F32 = jnp.float32
BF16 = jnp.bfloat16
ANY = pl.BlockSpec(memory_space=pl.ANY)
HBM = pl.BlockSpec(memory_space=pltpu.HBM)
VMEM = pl.BlockSpec(memory_space=pltpu.VMEM)
SMEM = pl.BlockSpec(memory_space=pltpu.SMEM)


def remote(src, dst, send_sem, recv_sem, device):
    return pltpu.make_async_remote_copy(
        src_ref=src,
        dst_ref=dst,
        send_sem=send_sem,
        recv_sem=recv_sem,
        device_id=device,
        device_id_type=MESH,
    )


def enter(rep, own, shards):
    barrier = pltpu.get_barrier_semaphore()

    @pl.loop(1, shards)
    def _(step):
        other = lax.rem(own + step, shards)
        pl.semaphore_signal(barrier, inc=1, device_id=(rep, other), device_id_type=MESH)

    for step in range(1, REP):
        other = lax.rem(rep + step, REP)
        pl.semaphore_signal(barrier, inc=1, device_id=(other, own), device_id_type=MESH)
    return lambda: pl.semaphore_wait(barrier, shards - 1 + REP - 1)


class RingGather:
    def __init__(self, out, first, count, rep, own, send_sems, recv_sems):
        self.send_sems, self.recv_sems = send_sems, recv_sems
        right, left = lax.rem(rep + 1, REP), lax.rem(rep + REP - 1, REP)
        far = lax.rem(rep + 2, REP)
        half = count // 2
        whole, front, back = pl.ds(first, count), pl.ds(first, half), pl.ds(first + half, half)
        to_right, to_left = (right, own), (left, own)
        self.sends = (
            self.copy(out.at[rep, whole], 0, to_right),
            self.copy(out.at[rep, whole], 1, to_left),
            self.copy(out.at[left, front], 2, to_right),
            self.copy(out.at[right, back], 3, to_left),
        )
        self.arrivals = (
            self.copy(out.at[left, whole], 0, to_right),
            self.copy(out.at[right, whole], 1, to_left),
            self.copy(out.at[far, front], 2, to_right),
            self.copy(out.at[far, back], 3, to_left),
        )

    def copy(self, piece, index, device):
        return remote(piece, piece, self.send_sems.at[index], self.recv_sems.at[index], device)

    def start(self):
        self.sends[0].start()
        self.sends[1].start()

    def forward(self):
        self.arrivals[0].wait_recv()
        self.sends[2].start()
        self.arrivals[1].wait_recv()
        self.sends[3].start()

    def finish(self):
        self.arrivals[2].wait_recv()
        self.arrivals[3].wait_recv()

    def sent(self):
        for send in self.sends:
            send.wait_send()


class Exchange:
    def __init__(self, shards, rep, own, source, target, send_sems, recv_sems):
        self.shards, self.rep, self.own = shards, rep, own
        self.source, self.target = source, target
        self.send_sems, self.recv_sems = send_sems, recv_sems
        self.size = shards // GROUPS

    def each(self, turn, body):
        group = lax.rem(self.own // self.size + turn, GROUPS)

        @pl.loop(1 if turn == 0 else 0, self.size)
        def _(step):
            body(group * self.size + lax.rem(self.own + step, self.size))

        return group * self.size

    def sent(self, other):
        return remote(
            self.source(other),
            self.target(self.own),
            self.send_sems.at[other],
            self.recv_sems.at[self.own],
            (self.rep, other),
        )

    def came(self, other):
        return remote(
            self.source(other),
            self.target(other),
            self.send_sems.at[other],
            self.recv_sems.at[other],
            (self.rep, other),
        )

    def start(self):
        for turn in TURNS:
            self.each(turn, lambda other: self.sent(other).start())

    def arrive(self, turn):
        return self.each(GROUPS - turn if turn else 0, lambda other: self.came(other).wait_recv())

    def finish(self):
        for turn in TURNS:
            self.each(turn, lambda other: self.sent(other).wait_send())


def gather_groups(exchange, out, kept, ring_sends, ring_recvs):
    rings = []
    for index, turn in enumerate(TURNS):
        first = exchange.arrive(turn)
        if turn == 0:
            kept.wait()
        ring = RingGather(
            out, first, exchange.size, exchange.rep, exchange.own, ring_sends.at[index], ring_recvs.at[index]
        )
        ring.start()
        if rings:
            rings[-1].forward()
        rings.append(ring)
    rings[-1].forward()
    for ring in rings:
        ring.finish()

    def sent():
        exchange.finish()
        for ring in rings:
            ring.sent()

    return sent


def product(left, right):
    return jnp.dot(left.astype(BF16), right.astype(BF16), preferred_element_type=F32)


def gradient(slots_ref, slot):
    count, shards, rows, width = slots_ref.shape
    columns = pl.ds(pl.multiple_of(slot * (width // 2), 128), width // 2)
    return jnp.concatenate(
        [
            slots_ref[index, :, :, columns].astype(F32).reshape(shards * rows, width // 2).astype(BF16)
            for index in range(count)
        ],
        axis=1,
    )


def outer(grad, side):
    axis = 1 - side
    return lax.dot_general(grad, grad, (((axis,), (axis,)), ((), ())), preferred_element_type=F32)


def step_kernel(
    shards,
    slot_ref,
    grad_ref,
    accum_ref,
    vocab_ref,
    left_ref,
    right_ref,
    slots_out,
    grad_out,
    vocab_out,
    rows_out,
    grad_own,
    grad_terms,
    grad_relay,
    grad_sum,
    accum_own,
    vocab_own,
    vocab_terms,
    vocab_sum,
    placement,
    outgoing,
    slots,
    graft_part,
    graft_parts,
    graft_totals,
    stats,
    scaled,
    result,
    mine,
    local_sems,
    grad_sends,
    grad_recvs,
    term_sends,
    term_recvs,
    slot_sends,
    slot_recvs,
    part_sends,
    part_recvs,
    row_sends,
    row_recvs,
    slot_ring_sends,
    slot_ring_recvs,
    row_ring_sends,
    row_ring_recvs,
    sum_ring_sends,
    sum_ring_recvs,
):
    rep, own = lax.axis_index("rep"), lax.axis_index("fsdp")
    right, left, far = (lax.rem(rep + step, REP) for step in (1, REP - 1, 2))
    to_right, to_left = (right, own), (left, own)
    pick, half = rep // 2, lax.rem(rep, 2)
    blocks, rows, quarter = grad_own.shape
    vocab_quarter = vocab_own.shape[-1]
    order = stats.shape[-1]

    def grad_columns(index):
        return pl.ds(pl.multiple_of(index * quarter, 128), quarter)

    def vocab_columns(index):
        return pl.ds(pl.multiple_of(index * vocab_quarter, 128), vocab_quarter)

    loads = (
        pltpu.make_async_copy(grad_ref.at[:, :, grad_columns(rep)], grad_own, local_sems.at[0]),
        pltpu.make_async_copy(accum_ref.at[:, :, grad_columns(rep)], accum_own, local_sems.at[1]),
        pltpu.make_async_copy(vocab_ref.at[:, :, vocab_columns(rep)], vocab_own, local_sems.at[2]),
        pltpu.make_async_copy(left_ref.at[pick], stats.at[0], local_sems.at[3]),
        pltpu.make_async_copy(right_ref.at[pick], stats.at[1], local_sems.at[4]),
    )
    entered = enter(rep, own, shards)
    for load in loads:
        load.start()

    total_rows = blocks * rows
    spread = jnp.where(
        lax.broadcasted_iota(jnp.int32, (blocks, total_rows), 0)
        == lax.broadcasted_iota(jnp.int32, (blocks, total_rows), 1) // rows,
        1.0,
        0.0,
    )
    slot_of = jnp.broadcast_to(slot_ref[...], (8, blocks)).astype(F32)
    slot_of = product(slot_of, spread)[:1].astype(jnp.int32)
    key = slot_of * rows + lax.rem(lax.broadcasted_iota(jnp.int32, (1, total_rows), 1), rows)
    key = jnp.broadcast_to(key, (shards * rows, total_rows))
    row = lax.broadcasted_iota(jnp.int32, (shards * rows, total_rows), 0)
    place = (row // rows) * (2 * rows) + lax.rem(row, rows)
    for slot in range(2):
        placement[slot] = jnp.where(key == place + slot * rows, 1.0, 0.0).astype(BF16)

    entered()
    front, back = pl.ds(0, blocks // 2), pl.ds(blocks // 2, blocks // 2)
    grad_pairs = (
        (grad_ref.at[front, :, grad_columns(far)], grad_relay.at[0], to_right),
        (grad_ref.at[back, :, grad_columns(far)], grad_relay.at[1], to_left),
        (grad_ref.at[:, :, grad_columns(right)], grad_terms.at[0], to_right),
        (grad_ref.at[:, :, grad_columns(left)], grad_terms.at[1], to_left),
        (grad_relay.at[0], grad_terms.at[2, front], to_right),
        (grad_relay.at[1], grad_terms.at[2, back], to_left),
    )
    grad_copies = [
        remote(source, target, grad_sends.at[index], grad_recvs.at[index], device)
        for index, (source, target, device) in enumerate(grad_pairs)
    ]
    for copy in grad_copies[:4]:
        copy.start()
    vocab_copies = []
    for step in range(1, REP):
        other = lax.rem(rep + step, REP)
        vocab_copies.append(
            remote(
                vocab_ref.at[:, :, vocab_columns(other)],
                vocab_terms.at[step - 1],
                term_sends.at[step - 1],
                term_recvs.at[step - 1],
                (other, own),
            )
        )
    for index in range(2):
        grad_copies[index].wait_recv()
        grad_copies[4 + index].start()
    loads[0].wait()
    for copy in grad_copies[2:]:
        copy.wait_recv()
    total = grad_own[...].astype(F32)
    for step in range(REP - 1):
        total = total + grad_terms[step].astype(F32)
    flat = total.reshape(total_rows, quarter).astype(BF16)
    for slot in range(2):
        placed = jnp.dot(placement[slot], flat, preferred_element_type=F32)
        outgoing[:, :, slot * quarter : (slot + 1) * quarter] = placed.reshape(
            shards, rows, quarter
        ).astype(BF16)
    slot_exchange = Exchange(
        shards,
        rep,
        own,
        lambda other: outgoing.at[other],
        lambda source: slots.at[rep, source],
        slot_sends,
        slot_recvs,
    )
    slot_exchange.start()
    keep = pltpu.make_async_copy(outgoing.at[own], slots.at[rep, own], local_sems.at[5])
    keep.start()
    for copy in vocab_copies:
        copy.start()
    grad_sum[...] = total.astype(BF16)
    keep_sum = pltpu.make_async_copy(grad_sum, grad_out.at[rep], local_sems.at[6])
    keep_sum.start()

    loads[1].wait()
    value = flat.astype(F32)
    accum_new = accum_own[...].reshape(total_rows, quarter) + value * value
    grafted = value / (jnp.sqrt(accum_new) + 1e-10)
    slot_count = 2 * shards
    slot = lax.broadcasted_iota(jnp.int32, (slot_count, total_rows), 0)
    chosen = jnp.where(jnp.broadcast_to(slot_of, (slot_count, total_rows)) == slot, 1.0, 0.0)
    by_slot = jnp.dot(chosen, grafted * grafted, precision=lax.Precision.HIGHEST)
    ones = jnp.ones((8, quarter), F32)
    parts = lax.dot_general(
        ones, by_slot, (((1,), (1,)), ((), ())), precision=lax.Precision.HIGHEST
    )
    graft_part[...] = parts[:1]
    graft_parts[pl.ds(own, 1)] = parts[:1][None]
    part_exchange = Exchange(
        shards,
        rep,
        own,
        lambda other: graft_part,
        lambda source: graft_parts.at[source],
        part_sends,
        part_recvs,
    )
    part_exchange.start()

    slots_sent = gather_groups(slot_exchange, slots, keep, slot_ring_sends, slot_ring_recvs)
    keep_slots = pltpu.make_async_copy(slots, slots_out, local_sems.at[7])
    keep_slots.start()

    keep_sum.wait()
    grad_ring = RingGather(grad_out, 0, blocks, rep, own, sum_ring_sends.at[0], sum_ring_recvs.at[0])
    grad_ring.start()
    loads[2].wait()
    for copy in vocab_copies:
        copy.wait_recv()
    vocab_total = vocab_own[...].astype(F32)
    for step in range(REP - 1):
        vocab_total = vocab_total + vocab_terms[step].astype(F32)
    vocab_sum[...] = vocab_total.astype(BF16)
    keep_vocab = pltpu.make_async_copy(vocab_sum, vocab_out.at[rep], local_sems.at[8])
    keep_vocab.start()

    for turn in TURNS:
        part_exchange.arrive(turn)
    graft_totals[pl.ds(rep, 1)] = jnp.sum(graft_parts[...], axis=0)[None]
    total_copies = []
    for step in range(1, REP):
        other, source = lax.rem(rep + step, REP), lax.rem(rep + REP - step, REP)
        index = REP - 1 + step - 1
        pieces = [graft_totals.at[pl.ds(place, 1)] for place in (rep, source)]
        total_copies.append(
            [remote(piece, piece, term_sends.at[index], term_recvs.at[index], (other, own)) for piece in pieces]
        )
        total_copies[-1][0].start()

    grad = gradient(slots, pick)
    row = lax.broadcasted_iota(jnp.int32, (order, order), 0)
    column = lax.broadcasted_iota(jnp.int32, (order, order), 1)
    for side in range(2):
        loads[3 + side].wait()
        matrix = stats[side] + outer(grad, side)
        start = matrix / jnp.sqrt(jnp.sum(matrix * matrix))
        scaled[side] = start
        result[side] = jnp.where(row == column, 1.25, 0.0) - 0.25 * start
    keep_vocab.wait()
    vocab_ring = RingGather(
        vocab_out, 0, vocab_own.shape[0], rep, own, sum_ring_sends.at[1], sum_ring_recvs.at[1]
    )
    vocab_ring.start()

    @pl.loop(1, ITERS)
    def _(iteration):
        for side in range(2):
            value = scaled[side]
            excess = product(value, value) * 0.0625 - 0.625 * value
            change = product(excess, excess) + 3.125 * excess
            value = product(change, value) + 2.44140625 * value
            scaled[side] = value
            root = result[side]
            result[side] = 1.25 * root - 0.25 * product(root, value)

        @pl.when(iteration == 2)
        def _():
            grad_ring.forward()
            vocab_ring.forward()

    shampoo = product(product(result[0], grad), result[1])
    for copy, arrival in total_copies:
        arrival.wait_recv()
    entries = float(order * order)
    lane = lax.broadcasted_iota(jnp.int32, (1, slot_count), 1)
    graft_total = jnp.sum(jnp.where(lane == 2 * own + pick, jnp.sum(graft_totals[...], axis=0), 0.0))
    graft_mean = jnp.full((1, 1), graft_total / entries, F32)
    shampoo_mean = jnp.full((1, 1), jnp.sum(shampoo * shampoo) / entries, F32)
    scale = jnp.sqrt(graft_mean) / jnp.sqrt(shampoo_mean + 1e-06)
    direction = shampoo * scale
    direction = jnp.where(half == 0, direction[:, : order // 2], direction[:, order // 2 :])
    mine[...] = direction.reshape(mine.shape).astype(BF16)
    row_exchange = Exchange(
        shards,
        rep,
        own,
        lambda other: mine.at[other],
        lambda source: rows_out.at[rep, source],
        row_sends,
        row_recvs,
    )
    row_exchange.start()
    keep_rows = pltpu.make_async_copy(mine.at[own], rows_out.at[rep, own], local_sems.at[9])
    keep_rows.start()
    grad_ring.finish()
    vocab_ring.finish()
    rows_sent = gather_groups(row_exchange, rows_out, keep_rows, row_ring_sends, row_ring_recvs)

    keep_slots.wait()
    for copy in grad_copies + vocab_copies:
        copy.wait_send()
    for copy, arrival in total_copies:
        copy.wait_send()
    part_exchange.finish()
    grad_ring.sent()
    vocab_ring.sent()
    slots_sent()
    rows_sent()


def shampoo_step(block_slot, grads, accum, vocab, left, right):
    shards = lax.axis_size("fsdp")
    blocks, rows, order = grads.shape
    quarter = order // REP
    vocab_shape = vocab.shape[:2] + (vocab.shape[-1] // REP,)
    row_shape = (REP, shards, rows, order // 2)
    dma = pltpu.SemaphoreType.DMA
    return pl.pallas_call(
        functools.partial(step_kernel, shards),
        out_shape=(
            jax.ShapeDtypeStruct(row_shape, BF16),
            jax.ShapeDtypeStruct((REP, blocks, rows, quarter), BF16),
            jax.ShapeDtypeStruct((REP,) + vocab_shape, BF16),
            jax.ShapeDtypeStruct(row_shape, BF16),
        ),
        in_specs=[VMEM, HBM, HBM, HBM, HBM, HBM],
        out_specs=(ANY, ANY, ANY, ANY),
        scratch_shapes=[
            pltpu.VMEM((blocks, rows, quarter), BF16),
            pltpu.VMEM((REP - 1, blocks, rows, quarter), BF16),
            pltpu.VMEM((2, blocks // 2, rows, quarter), BF16),
            pltpu.VMEM((blocks, rows, quarter), BF16),
            pltpu.VMEM((blocks, rows, quarter), F32),
            pltpu.VMEM(vocab_shape, BF16),
            pltpu.VMEM((REP - 1,) + vocab_shape, BF16),
            pltpu.VMEM(vocab_shape, BF16),
            pltpu.VMEM((2, shards * rows, blocks * rows), BF16),
            pltpu.VMEM(row_shape[1:], BF16),
            pltpu.VMEM(row_shape, BF16),
            pltpu.VMEM((1, 2 * shards), F32),
            pltpu.VMEM((shards, 1, 2 * shards), F32),
            pltpu.VMEM((REP, 1, 2 * shards), F32),
            pltpu.VMEM((2, order, order), F32),
            pltpu.VMEM((2, order, order), F32),
            pltpu.VMEM((2, order, order), F32),
            pltpu.VMEM(row_shape[1:], BF16),
            dma((10,)),
            dma((6,)),
            dma((6,)),
            dma((2 * (REP - 1),)),
            dma((2 * (REP - 1),)),
            dma((shards,)),
            dma((shards,)),
            dma((shards,)),
            dma((shards,)),
            dma((shards,)),
            dma((shards,)),
            dma((GROUPS, 4)),
            dma((GROUPS, 4)),
            dma((GROUPS, 4)),
            dma((GROUPS, 4)),
            dma((2, 4)),
            dma((2, 4)),
        ],
        compiler_params=pltpu.CompilerParams(
            collective_id=0, has_side_effects=True, vmem_limit_bytes=30 * 1024 * 1024
        ),
        name="shampoo_step",
    )(
        block_slot.reshape(1, -1),
        *(pltpu.with_memory_space_constraint(array, pltpu.HBM) for array in (grads, accum, vocab, left, right)),
    )


def finish_kernel(
    slot_ref,
    slots_ref,
    grad_ref,
    vocab_ref,
    rows_ref,
    accum_ref,
    left_ref,
    right_ref,
    vocab_accum_ref,
    direction_out,
    accum_out,
    left_out,
    right_out,
    vocab_out,
    step_out,
):
    half = rows_ref.shape[-1]
    for slot in range(2):
        grad = gradient(slots_ref, slot)
        for side, (ref, out) in enumerate(((left_ref, left_out), (right_ref, right_out))):
            out[slot] = ref[slot] + outer(grad, side)
    for index in range(REP):
        quarter, vocab_quarter = grad_ref.shape[-1], vocab_ref.shape[-1]
        columns = slice(index * quarter, (index + 1) * quarter)
        grad = grad_ref[index].astype(F32)
        accum_out[:, :, columns] = accum_ref[:, :, columns] + grad * grad
        columns = slice(index * vocab_quarter, (index + 1) * vocab_quarter)
        vocab = vocab_ref[index].astype(F32)
        vocab_accum = vocab_accum_ref[:, :, columns] + vocab * vocab
        vocab_out[:, :, columns] = vocab_accum
        step_out[:, :, columns] = (vocab / (jnp.sqrt(vocab_accum) + 1e-10)).astype(BF16)

    @pl.loop(0, direction_out.shape[0])
    def _(block):
        slot = slot_ref[block]
        owner, pick = slot // 2, lax.rem(slot, 2)
        for side in range(2):
            direction_out[block, :, side * half : (side + 1) * half] = rows_ref[2 * pick + side, owner]


def finish(block_slot, slots, grads, vocab, rows, accum, left, right, vocab_accum):
    direction = (block_slot.shape[0], rows.shape[2], 2 * rows.shape[3])
    return pl.pallas_call(
        finish_kernel,
        out_shape=(
            jax.ShapeDtypeStruct(direction, BF16),
            jax.ShapeDtypeStruct(accum.shape, F32),
            jax.ShapeDtypeStruct(left.shape, F32),
            jax.ShapeDtypeStruct(right.shape, F32),
            jax.ShapeDtypeStruct(vocab_accum.shape, F32),
            jax.ShapeDtypeStruct(vocab_accum.shape, BF16),
        ),
        in_specs=[SMEM] + [VMEM] * 8,
        out_specs=(VMEM,) * 6,
        compiler_params=pltpu.CompilerParams(vmem_limit_bytes=30 * 1024 * 1024),
        name="finish",
    )(block_slot, slots, grads, vocab, rows, accum, left, right, vocab_accum)


def on_device(
    grad_blocks, graft_accum, left_stats, right_stats, block_slot, vocab_grads, vocab_accum
):
    slots, grads, vocab, rows = shampoo_step(
        block_slot, grad_blocks[0], graft_accum, vocab_grads[0], left_stats, right_stats
    )
    return finish(
        block_slot, slots, grads, vocab, rows, graft_accum, left_stats, right_stats, vocab_accum
    )


def solution(mesh):
    in_specs = (
        P("rep", None, "fsdp", None),
        P(None, "fsdp", None),
        P("fsdp", None, None),
        P("fsdp", None, None),
        P(),
        P("rep", None, "fsdp", None),
        P(None, "fsdp", None),
    )
    out_specs = (
        P(None, "fsdp", None),
        P(None, "fsdp", None),
        P("fsdp", None, None),
        P("fsdp", None, None),
        P(None, "fsdp", None),
        P(None, "fsdp", None),
    )
    return jax.shard_map(
        on_device, mesh=mesh, in_specs=in_specs, out_specs=out_specs, check_vma=False
    )
```

```python
import functools

import jax
import jax.numpy as jnp
from jax import lax
from jax.experimental import pallas as pl
from jax.experimental.pallas import tpu as pltpu
from jax.sharding import PartitionSpec as P

ITERS = 6
REP = 4
GROUPS = 4
TURNS = (0, 1, 3, 2)
MESH = pl.DeviceIdType.MESH
F32 = jnp.float32
BF16 = jnp.bfloat16
ANY = pl.BlockSpec(memory_space=pl.ANY)
HBM = pl.BlockSpec(memory_space=pltpu.HBM)
VMEM = pl.BlockSpec(memory_space=pltpu.VMEM)
SMEM = pl.BlockSpec(memory_space=pltpu.SMEM)


def remote(src, dst, send_sem, recv_sem, device):
    return pltpu.make_async_remote_copy(
        src_ref=src,
        dst_ref=dst,
        send_sem=send_sem,
        recv_sem=recv_sem,
        device_id=device,
        device_id_type=MESH,
    )


def enter(rep, own, shards):
    barrier = pltpu.get_barrier_semaphore()

    @pl.loop(1, shards)
    def _(step):
        other = lax.rem(own + step, shards)
        pl.semaphore_signal(barrier, inc=1, device_id=(rep, other), device_id_type=MESH)

    for step in range(1, REP):
        other = lax.rem(rep + step, REP)
        pl.semaphore_signal(barrier, inc=1, device_id=(other, own), device_id_type=MESH)
    return lambda: pl.semaphore_wait(barrier, shards - 1 + REP - 1)


class RingGather:
    def __init__(self, out, first, count, rep, own, send_sems, recv_sems):
        self.send_sems, self.recv_sems = send_sems, recv_sems
        right, left = lax.rem(rep + 1, REP), lax.rem(rep + REP - 1, REP)
        far = lax.rem(rep + 2, REP)
        half = count // 2
        whole, front, back = pl.ds(first, count), pl.ds(first, half), pl.ds(first + half, half)
        to_right, to_left = (right, own), (left, own)
        self.sends = (
            self.copy(out.at[rep, whole], 0, to_right),
            self.copy(out.at[rep, whole], 1, to_left),
            self.copy(out.at[left, front], 2, to_right),
            self.copy(out.at[right, back], 3, to_left),
        )
        self.arrivals = (
            self.copy(out.at[left, whole], 0, to_right),
            self.copy(out.at[right, whole], 1, to_left),
            self.copy(out.at[far, front], 2, to_right),
            self.copy(out.at[far, back], 3, to_left),
        )

    def copy(self, piece, index, device):
        return remote(piece, piece, self.send_sems.at[index], self.recv_sems.at[index], device)

    def start(self):
        self.sends[0].start()
        self.sends[1].start()

    def forward(self):
        self.arrivals[0].wait_recv()
        self.sends[2].start()
        self.arrivals[1].wait_recv()
        self.sends[3].start()

    def finish(self):
        self.arrivals[2].wait_recv()
        self.arrivals[3].wait_recv()

    def sent(self):
        for send in self.sends:
            send.wait_send()


class PairGather:
    def __init__(self, slots, first, count, rep, own, send_sems, recv_sems):
        self.send_sems, self.recv_sems = send_sems, recv_sems
        odd = lax.rem(rep, 2)
        partner, beside = rep + 1 - 2 * odd, lax.rem(rep + 3 + 2 * odd, REP)
        far = lax.rem(rep + 2, REP)
        pick, rows = rep // 2, pl.ds(first, count)
        other = 1 - pick
        to_partner, to_beside = (partner, own), (beside, own)

        def copy(slot, index, sem, device):
            piece = slots.at[slot, index, rows]
            return remote(piece, piece, send_sems.at[sem], recv_sems.at[sem], device)

        self.sends = (
            copy(pick, rep, 0, to_partner),
            copy(other, rep, 1, to_beside),
            copy(pick, beside, 2, to_partner),
        )
        self.arrivals = (
            copy(pick, partner, 0, to_partner),
            copy(pick, beside, 1, to_beside),
            copy(pick, far, 2, to_partner),
        )
        self.rest = (
            copy(other, rep, 3, to_partner),
            copy(pick, rep, 4, to_beside),
            copy(pick, partner, 5, to_beside),
        )
        self.rest_arrivals = (
            copy(other, partner, 3, to_partner),
            copy(other, beside, 4, to_beside),
            copy(other, far, 5, to_beside),
        )

    def start(self):
        self.sends[0].start()
        self.sends[1].start()

    def forward(self):
        self.arrivals[1].wait_recv()
        self.sends[2].start()

    def finish(self):
        self.arrivals[0].wait_recv()
        self.arrivals[2].wait_recv()

    def sent(self):
        for send in self.sends:
            send.wait_send()

    def start_rest(self):
        for send in self.rest:
            send.start()

    def finish_rest(self):
        for arrival in self.rest_arrivals:
            arrival.wait_recv()
        for send in self.rest:
            send.wait_send()


class Exchange:
    def __init__(self, shards, rep, own, source, target, send_sems, recv_sems):
        self.shards, self.rep, self.own = shards, rep, own
        self.source, self.target = source, target
        self.send_sems, self.recv_sems = send_sems, recv_sems
        self.size = shards // GROUPS

    def each(self, turn, body):
        group = lax.rem(self.own // self.size + turn, GROUPS)

        @pl.loop(1 if turn == 0 else 0, self.size)
        def _(step):
            body(group * self.size + lax.rem(self.own + step, self.size))

        return group * self.size

    def sent(self, other):
        return remote(
            self.source(other),
            self.target(self.own),
            self.send_sems.at[other],
            self.recv_sems.at[self.own],
            (self.rep, other),
        )

    def came(self, other):
        return remote(
            self.source(other),
            self.target(other),
            self.send_sems.at[other],
            self.recv_sems.at[other],
            (self.rep, other),
        )

    def start(self):
        for turn in TURNS:
            self.each(turn, lambda other: self.sent(other).start())

    def arrive(self, turn):
        return self.each(GROUPS - turn if turn else 0, lambda other: self.came(other).wait_recv())

    def finish(self):
        for turn in TURNS:
            self.each(turn, lambda other: self.sent(other).wait_send())


def gather_groups(ring_type, exchange, out, kept, ring_sends, ring_recvs):
    rings = []
    for index, turn in enumerate(TURNS):
        first = exchange.arrive(turn)
        if turn == 0:
            kept.wait()
        ring = ring_type(
            out, first, exchange.size, exchange.rep, exchange.own, ring_sends.at[index], ring_recvs.at[index]
        )
        ring.start()
        if rings:
            rings[-1].forward()
        rings.append(ring)
    rings[-1].forward()
    for ring in rings:
        ring.finish()

    def sent():
        exchange.finish()
        for ring in rings:
            ring.sent()

    return sent


def product(left, right):
    return jnp.dot(left.astype(BF16), right.astype(BF16), preferred_element_type=F32)


def gradient(slots_ref, slot):
    count, shards, rows, quarter = slots_ref.shape[1:]
    return jnp.concatenate(
        [
            slots_ref[slot, index].astype(F32).reshape(shards * rows, quarter).astype(BF16)
            for index in range(count)
        ],
        axis=1,
    )


def outer(grad, side):
    axis = 1 - side
    return lax.dot_general(grad, grad, (((axis,), (axis,)), ((), ())), preferred_element_type=F32)


def step_kernel(
    shards,
    slot_ref,
    grad_ref,
    accum_ref,
    vocab_ref,
    left_ref,
    right_ref,
    slots_out,
    grad_out,
    vocab_out,
    rows_out,
    slot_own,
    grad_own,
    grad_terms,
    grad_relay,
    grad_sum,
    accum_own,
    vocab_own,
    vocab_terms,
    vocab_sum,
    placement,
    outgoing,
    slots,
    graft_part,
    graft_parts,
    graft_totals,
    stats,
    scaled,
    result,
    mine,
    local_sems,
    grad_sends,
    grad_recvs,
    term_sends,
    term_recvs,
    slot_sends,
    slot_recvs,
    part_sends,
    part_recvs,
    row_sends,
    row_recvs,
    slot_ring_sends,
    slot_ring_recvs,
    row_ring_sends,
    row_ring_recvs,
    sum_ring_sends,
    sum_ring_recvs,
    slot_rest_sems,
):
    rep, own = lax.axis_index("rep"), lax.axis_index("fsdp")
    right, left, far = (lax.rem(rep + step, REP) for step in (1, REP - 1, 2))
    to_right, to_left = (right, own), (left, own)
    pick, half = rep // 2, lax.rem(rep, 2)
    blocks, rows, quarter = grad_own.shape
    vocab_quarter = vocab_own.shape[-1]
    order = stats.shape[-1]

    def grad_columns(index):
        return pl.ds(pl.multiple_of(index * quarter, 128), quarter)

    def vocab_columns(index):
        return pl.ds(pl.multiple_of(index * vocab_quarter, 128), vocab_quarter)

    loads = (
        pltpu.make_async_copy(grad_ref.at[:, :, grad_columns(rep)], grad_own, local_sems.at[0]),
        pltpu.make_async_copy(accum_ref.at[:, :, grad_columns(rep)], accum_own, local_sems.at[1]),
        pltpu.make_async_copy(vocab_ref.at[:, :, vocab_columns(rep)], vocab_own, local_sems.at[2]),
        pltpu.make_async_copy(left_ref.at[pick], stats.at[0], local_sems.at[3]),
        pltpu.make_async_copy(right_ref.at[pick], stats.at[1], local_sems.at[4]),
    )
    load_slot = pltpu.make_async_copy(slot_ref, slot_own, local_sems.at[10])
    load_slot.start()
    entered = enter(rep, own, shards)
    for load in loads:
        load.start()

    total_rows = blocks * rows
    spread = jnp.where(
        lax.broadcasted_iota(jnp.int32, (blocks, total_rows), 0)
        == lax.broadcasted_iota(jnp.int32, (blocks, total_rows), 1) // rows,
        1.0,
        0.0,
    )
    load_slot.wait()
    slot_of = jnp.broadcast_to(slot_own[...], (8, blocks)).astype(F32)
    slot_of = product(slot_of, spread)[:1].astype(jnp.int32)
    key = slot_of * rows + lax.rem(lax.broadcasted_iota(jnp.int32, (1, total_rows), 1), rows)
    key = jnp.broadcast_to(key, (shards * rows, total_rows))
    row = lax.broadcasted_iota(jnp.int32, (shards * rows, total_rows), 0)
    place = (row // rows) * (2 * rows) + lax.rem(row, rows)
    for slot in range(2):
        placement[slot] = jnp.where(key == place + slot * rows, 1.0, 0.0).astype(BF16)

    entered()
    front, back = pl.ds(0, blocks // 2), pl.ds(blocks // 2, blocks // 2)
    grad_pairs = (
        (grad_ref.at[front, :, grad_columns(far)], grad_relay.at[0], to_right),
        (grad_ref.at[back, :, grad_columns(far)], grad_relay.at[1], to_left),
        (grad_ref.at[:, :, grad_columns(right)], grad_terms.at[0], to_right),
        (grad_ref.at[:, :, grad_columns(left)], grad_terms.at[1], to_left),
        (grad_relay.at[0], grad_terms.at[2, front], to_right),
        (grad_relay.at[1], grad_terms.at[2, back], to_left),
    )
    grad_copies = [
        remote(source, target, grad_sends.at[index], grad_recvs.at[index], device)
        for index, (source, target, device) in enumerate(grad_pairs)
    ]
    for copy in grad_copies[:4]:
        copy.start()
    vocab_copies = []
    for step in range(1, REP):
        other = lax.rem(rep + step, REP)
        vocab_copies.append(
            remote(
                vocab_ref.at[:, :, vocab_columns(other)],
                vocab_terms.at[step - 1],
                term_sends.at[step - 1],
                term_recvs.at[step - 1],
                (other, own),
            )
        )
    for index in range(2):
        grad_copies[index].wait_recv()
        grad_copies[4 + index].start()
    loads[0].wait()
    for copy in grad_copies[2:]:
        copy.wait_recv()
    total = grad_own[...].astype(F32)
    for step in range(REP - 1):
        total = total + grad_terms[step].astype(F32)
    flat = total.reshape(total_rows, quarter).astype(BF16)
    for slot in range(2):
        placed = jnp.dot(placement[slot], flat, preferred_element_type=F32)
        outgoing[:, slot] = placed.reshape(shards, rows, quarter).astype(BF16)
    slot_exchange = Exchange(
        shards,
        rep,
        own,
        lambda other: outgoing.at[other],
        lambda source: slots.at[:, rep, source],
        slot_sends,
        slot_recvs,
    )
    slot_exchange.start()
    keep = pltpu.make_async_copy(outgoing.at[own], slots.at[:, rep, own], local_sems.at[5])
    keep.start()
    for copy in vocab_copies:
        copy.start()
    grad_sum[...] = total.astype(BF16)
    keep_sum = pltpu.make_async_copy(grad_sum, grad_out.at[rep], local_sems.at[6])
    keep_sum.start()

    loads[1].wait()
    value = flat.astype(F32)
    accum_new = accum_own[...].reshape(total_rows, quarter) + value * value
    grafted = value / (jnp.sqrt(accum_new) + 1e-10)
    slot_count = 2 * shards
    slot = lax.broadcasted_iota(jnp.int32, (slot_count, total_rows), 0)
    chosen = jnp.where(jnp.broadcast_to(slot_of, (slot_count, total_rows)) == slot, 1.0, 0.0)
    by_slot = jnp.dot(chosen, grafted * grafted, precision=lax.Precision.HIGHEST)
    ones = jnp.ones((8, quarter), F32)
    parts = lax.dot_general(
        ones, by_slot, (((1,), (1,)), ((), ())), precision=lax.Precision.HIGHEST
    )
    graft_part[...] = parts[:1]
    graft_parts[pl.ds(own, 1)] = parts[:1][None]
    part_exchange = Exchange(
        shards,
        rep,
        own,
        lambda other: graft_part,
        lambda source: graft_parts.at[source],
        part_sends,
        part_recvs,
    )
    part_exchange.start()

    slots_sent = gather_groups(PairGather, slot_exchange, slots, keep, slot_ring_sends, slot_ring_recvs)
    slot_rest = PairGather(slots, 0, shards, rep, own, slot_rest_sems.at[0], slot_rest_sems.at[1])
    slot_rest.start_rest()
    keep_sum.wait()
    grad_ring = RingGather(grad_out, 0, blocks, rep, own, sum_ring_sends.at[0], sum_ring_recvs.at[0])
    grad_ring.start()
    keep_vocab = pltpu.make_async_copy(vocab_sum, vocab_out.at[rep], local_sems.at[8])
    vocab_ring = RingGather(
        vocab_out, 0, vocab_own.shape[0], rep, own, sum_ring_sends.at[1], sum_ring_recvs.at[1]
    )
    total_copies = []
    for step in range(1, REP):
        other, source = lax.rem(rep + step, REP), lax.rem(rep + REP - step, REP)
        index = REP - 1 + step - 1
        pieces = [graft_totals.at[pl.ds(place, 1)] for place in (rep, source)]
        total_copies.append(
            [remote(piece, piece, term_sends.at[index], term_recvs.at[index], (other, own)) for piece in pieces]
        )

    grad = gradient(slots, pick)
    row = lax.broadcasted_iota(jnp.int32, (order, order), 0)
    column = lax.broadcasted_iota(jnp.int32, (order, order), 1)
    for side in range(2):
        loads[3 + side].wait()
        matrix = stats[side] + outer(grad, side)
        start = matrix / jnp.sqrt(jnp.sum(matrix * matrix))
        scaled[side] = start
        result[side] = jnp.where(row == column, 1.25, 0.0) - 0.25 * start

    @pl.loop(1, ITERS)
    def _(iteration):
        for side in range(2):
            value = scaled[side]
            excess = product(value, value) * 0.0625 - 0.625 * value
            change = product(excess, excess) + 3.125 * excess
            value = product(change, value) + 2.44140625 * value
            scaled[side] = value
            root = result[side]
            result[side] = 1.25 * root - 0.25 * product(root, value)

        @pl.when(iteration == 2)
        def _():
            for turn in TURNS:
                part_exchange.arrive(turn)
            graft_totals[pl.ds(rep, 1)] = jnp.sum(graft_parts[...], axis=0)[None]
            for copy, arrival in total_copies:
                copy.start()
            loads[2].wait()
            for copy in vocab_copies:
                copy.wait_recv()
            vocab_total = vocab_own[...].astype(F32)
            for step in range(REP - 1):
                vocab_total = vocab_total + vocab_terms[step].astype(F32)
            vocab_sum[...] = vocab_total.astype(BF16)
            keep_vocab.start()

        @pl.when(iteration == 3)
        def _():
            keep_vocab.wait()
            vocab_ring.start()
            grad_ring.forward()

    shampoo = product(product(result[0], grad), result[1])
    for copy, arrival in total_copies:
        arrival.wait_recv()
    entries = float(order * order)
    lane = lax.broadcasted_iota(jnp.int32, (1, slot_count), 1)
    graft_total = jnp.sum(jnp.where(lane == 2 * own + pick, jnp.sum(graft_totals[...], axis=0), 0.0))
    graft_mean = jnp.full((1, 1), graft_total / entries, F32)
    shampoo_mean = jnp.full((1, 1), jnp.sum(shampoo * shampoo) / entries, F32)
    scale = jnp.sqrt(graft_mean) / jnp.sqrt(shampoo_mean + 1e-06)
    direction = shampoo * scale
    direction = jnp.where(half == 0, direction[:, : order // 2], direction[:, order // 2 :])
    mine[...] = direction.reshape(mine.shape).astype(BF16)
    row_exchange = Exchange(
        shards,
        rep,
        own,
        lambda other: mine.at[other],
        lambda source: rows_out.at[rep, source],
        row_sends,
        row_recvs,
    )
    row_exchange.start()
    keep_rows = pltpu.make_async_copy(mine.at[own], rows_out.at[rep, own], local_sems.at[9])
    keep_rows.start()
    vocab_ring.forward()
    slot_rest.finish_rest()
    keep_slots = pltpu.make_async_copy(slots, slots_out, local_sems.at[7])
    keep_slots.start()
    rows_sent = gather_groups(RingGather, row_exchange, rows_out, keep_rows, row_ring_sends, row_ring_recvs)

    grad_ring.finish()
    vocab_ring.finish()
    keep_slots.wait()
    for copy in grad_copies + vocab_copies:
        copy.wait_send()
    for copy, arrival in total_copies:
        copy.wait_send()
    part_exchange.finish()
    grad_ring.sent()
    vocab_ring.sent()
    slots_sent()
    rows_sent()


def shampoo_step(block_slot, grads, accum, vocab, left, right):
    shards = lax.axis_size("fsdp")
    blocks, rows, order = grads.shape
    quarter = order // REP
    vocab_shape = vocab.shape[:2] + (vocab.shape[-1] // REP,)
    row_shape = (REP, shards, rows, order // 2)
    slot_shape = (2, REP, shards, rows, quarter)
    dma = pltpu.SemaphoreType.DMA
    return pl.pallas_call(
        functools.partial(step_kernel, shards),
        out_shape=(
            jax.ShapeDtypeStruct(slot_shape, BF16),
            jax.ShapeDtypeStruct((REP, blocks, rows, quarter), BF16),
            jax.ShapeDtypeStruct((REP,) + vocab_shape, BF16),
            jax.ShapeDtypeStruct(row_shape, BF16),
        ),
        in_specs=[HBM] * 6,
        out_specs=(ANY, ANY, ANY, ANY),
        scratch_shapes=[
            pltpu.VMEM((1, blocks), jnp.int32),
            pltpu.VMEM((blocks, rows, quarter), BF16),
            pltpu.VMEM((REP - 1, blocks, rows, quarter), BF16),
            pltpu.VMEM((2, blocks // 2, rows, quarter), BF16),
            pltpu.VMEM((blocks, rows, quarter), BF16),
            pltpu.VMEM((blocks, rows, quarter), F32),
            pltpu.VMEM(vocab_shape, BF16),
            pltpu.VMEM((REP - 1,) + vocab_shape, BF16),
            pltpu.VMEM(vocab_shape, BF16),
            pltpu.VMEM((2, shards * rows, blocks * rows), BF16),
            pltpu.VMEM((shards, 2, rows, quarter), BF16),
            pltpu.VMEM(slot_shape, BF16),
            pltpu.VMEM((1, 2 * shards), F32),
            pltpu.VMEM((shards, 1, 2 * shards), F32),
            pltpu.VMEM((REP, 1, 2 * shards), F32),
            pltpu.VMEM((2, order, order), F32),
            pltpu.VMEM((2, order, order), F32),
            pltpu.VMEM((2, order, order), F32),
            pltpu.VMEM(row_shape[1:], BF16),
            dma((11,)),
            dma((6,)),
            dma((6,)),
            dma((2 * (REP - 1),)),
            dma((2 * (REP - 1),)),
            dma((shards,)),
            dma((shards,)),
            dma((shards,)),
            dma((shards,)),
            dma((shards,)),
            dma((shards,)),
            dma((GROUPS, 6)),
            dma((GROUPS, 6)),
            dma((GROUPS, 4)),
            dma((GROUPS, 4)),
            dma((2, 4)),
            dma((2, 4)),
            dma((2, 6)),
        ],
        compiler_params=pltpu.CompilerParams(
            collective_id=0, has_side_effects=True, vmem_limit_bytes=30 * 1024 * 1024
        ),
        name="shampoo_step",
    )(
        *(
            pltpu.with_memory_space_constraint(array, pltpu.HBM)
            for array in (block_slot.reshape(1, -1), grads, accum, vocab, left, right)
        )
    )


def finish_kernel(
    slot_ref,
    slots_ref,
    grad_ref,
    vocab_ref,
    rows_ref,
    accum_ref,
    left_ref,
    right_ref,
    vocab_accum_ref,
    direction_out,
    accum_out,
    left_out,
    right_out,
    vocab_out,
    step_out,
    direction,
    accum,
    stats,
    vocab_accum,
    vocab_step,
    sems,
):
    half = rows_ref.shape[-1]
    stores = []

    def store(source, target):
        stores.append(pltpu.make_async_copy(source, target, sems.at[len(stores)]))
        stores[-1].start()

    for slot in range(2):
        grad = gradient(slots_ref, slot)
        for side, (ref, out) in enumerate(((left_ref, left_out), (right_ref, right_out))):
            stats[side, slot] = ref[slot] + outer(grad, side)
            store(stats.at[side, slot], out.at[slot])
    for index in range(REP):
        quarter = grad_ref.shape[-1]
        columns = slice(index * quarter, (index + 1) * quarter)
        grad = grad_ref[index].astype(F32)
        accum[:, :, columns] = accum_ref[:, :, columns] + grad * grad
    store(accum, accum_out)
    for index in range(REP):
        quarter = vocab_ref.shape[-1]
        columns = slice(index * quarter, (index + 1) * quarter)
        vocab = vocab_ref[index].astype(F32)
        value = vocab_accum_ref[:, :, columns] + vocab * vocab
        vocab_accum[:, :, columns] = value
        vocab_step[:, :, columns] = (vocab / (jnp.sqrt(value) + 1e-10)).astype(BF16)
    store(vocab_accum, vocab_out)
    store(vocab_step, step_out)

    @pl.loop(0, direction.shape[0], unroll=4)
    def _(block):
        slot = slot_ref[block]
        owner, pick = slot // 2, lax.rem(slot, 2)
        for side in range(2):
            direction[block, :, side * half : (side + 1) * half] = rows_ref[2 * pick + side, owner]

    store(direction, direction_out)
    for copy in stores:
        copy.wait()


def finish(block_slot, slots, grads, vocab, rows, accum, left, right, vocab_accum):
    direction = (block_slot.shape[0], rows.shape[2], 2 * rows.shape[3])
    return pl.pallas_call(
        finish_kernel,
        out_shape=(
            jax.ShapeDtypeStruct(direction, BF16),
            jax.ShapeDtypeStruct(accum.shape, F32),
            jax.ShapeDtypeStruct(left.shape, F32),
            jax.ShapeDtypeStruct(right.shape, F32),
            jax.ShapeDtypeStruct(vocab_accum.shape, F32),
            jax.ShapeDtypeStruct(vocab_accum.shape, BF16),
        ),
        in_specs=[SMEM] + [VMEM] * 8,
        out_specs=(HBM,) * 6,
        scratch_shapes=[
            pltpu.VMEM(direction, BF16),
            pltpu.VMEM(accum.shape, F32),
            pltpu.VMEM((2,) + left.shape, F32),
            pltpu.VMEM(vocab_accum.shape, F32),
            pltpu.VMEM(vocab_accum.shape, BF16),
            pltpu.SemaphoreType.DMA((8,)),
        ],
        compiler_params=pltpu.CompilerParams(vmem_limit_bytes=30 * 1024 * 1024),
        name="finish",
    )(block_slot, slots, grads, vocab, rows, accum, left, right, vocab_accum)


def on_device(
    grad_blocks, graft_accum, left_stats, right_stats, block_slot, vocab_grads, vocab_accum
):
    slots, grads, vocab, rows = shampoo_step(
        block_slot, grad_blocks[0], graft_accum, vocab_grads[0], left_stats, right_stats
    )
    return finish(
        block_slot, slots, grads, vocab, rows, graft_accum, left_stats, right_stats, vocab_accum
    )


def solution(mesh):
    in_specs = (
        P("rep", None, "fsdp", None),
        P(None, "fsdp", None),
        P("fsdp", None, None),
        P("fsdp", None, None),
        P(),
        P("rep", None, "fsdp", None),
        P(None, "fsdp", None),
    )
    out_specs = (
        P(None, "fsdp", None),
        P(None, "fsdp", None),
        P("fsdp", None, None),
        P("fsdp", None, None),
        P(None, "fsdp", None),
        P(None, "fsdp", None),
    )
    return jax.shard_map(
        on_device, mesh=mesh, in_specs=in_specs, out_specs=out_specs, check_vma=False
    )
```

```python
import functools

import jax
import jax.numpy as jnp
from jax import lax
from jax.experimental import pallas as pl
from jax.experimental.pallas import tpu as pltpu
from jax.sharding import PartitionSpec as P

ITERS = 6
REP = 4
GROUPS = 4
TURNS = (0, 1, 3, 2)
MESH = pl.DeviceIdType.MESH
F32 = jnp.float32
BF16 = jnp.bfloat16
ANY = pl.BlockSpec(memory_space=pl.ANY)
HBM = pl.BlockSpec(memory_space=pltpu.HBM)
VMEM = pl.BlockSpec(memory_space=pltpu.VMEM)
SMEM = pl.BlockSpec(memory_space=pltpu.SMEM)


def remote(src, dst, send_sem, recv_sem, device):
    return pltpu.make_async_remote_copy(
        src_ref=src,
        dst_ref=dst,
        send_sem=send_sem,
        recv_sem=recv_sem,
        device_id=device,
        device_id_type=MESH,
    )


def enter(rep, own, shards):
    barrier = pltpu.get_barrier_semaphore()

    @pl.loop(1, shards)
    def _(step):
        other = lax.rem(own + step, shards)
        pl.semaphore_signal(barrier, inc=1, device_id=(rep, other), device_id_type=MESH)

    for step in range(1, REP):
        other = lax.rem(rep + step, REP)
        pl.semaphore_signal(barrier, inc=1, device_id=(other, own), device_id_type=MESH)
    return lambda: pl.semaphore_wait(barrier, shards - 1 + REP - 1)


class RingGather:
    def __init__(self, out, first, count, rep, own, send_sems, recv_sems):
        self.send_sems, self.recv_sems = send_sems, recv_sems
        right, left = lax.rem(rep + 1, REP), lax.rem(rep + REP - 1, REP)
        far = lax.rem(rep + 2, REP)
        half = count // 2
        whole, front, back = pl.ds(first, count), pl.ds(first, half), pl.ds(first + half, half)
        to_right, to_left = (right, own), (left, own)
        self.sends = (
            self.copy(out.at[rep, whole], 0, to_right),
            self.copy(out.at[rep, whole], 1, to_left),
            self.copy(out.at[left, front], 2, to_right),
            self.copy(out.at[right, back], 3, to_left),
        )
        self.arrivals = (
            self.copy(out.at[left, whole], 0, to_right),
            self.copy(out.at[right, whole], 1, to_left),
            self.copy(out.at[far, front], 2, to_right),
            self.copy(out.at[far, back], 3, to_left),
        )

    def copy(self, piece, index, device):
        return remote(piece, piece, self.send_sems.at[index], self.recv_sems.at[index], device)

    def start(self):
        self.sends[0].start()
        self.sends[1].start()

    def forward(self):
        self.arrivals[0].wait_recv()
        self.sends[2].start()
        self.arrivals[1].wait_recv()
        self.sends[3].start()

    def finish(self):
        self.arrivals[2].wait_recv()
        self.arrivals[3].wait_recv()

    def sent(self):
        for send in self.sends:
            send.wait_send()


class PairGather:
    def __init__(self, slots, first, count, rep, own, send_sems, recv_sems):
        self.send_sems, self.recv_sems = send_sems, recv_sems
        odd = lax.rem(rep, 2)
        partner, beside = rep + 1 - 2 * odd, lax.rem(rep + 3 + 2 * odd, REP)
        far = lax.rem(rep + 2, REP)
        pick, rows = rep // 2, pl.ds(first, count)
        other = 1 - pick
        to_partner, to_beside = (partner, own), (beside, own)

        def copy(slot, index, sem, device):
            piece = slots.at[slot, index, rows]
            return remote(piece, piece, send_sems.at[sem], recv_sems.at[sem], device)

        self.sends = (
            copy(pick, rep, 0, to_partner),
            copy(other, rep, 1, to_beside),
            copy(pick, beside, 2, to_partner),
        )
        self.arrivals = (
            copy(pick, partner, 0, to_partner),
            copy(pick, beside, 1, to_beside),
            copy(pick, far, 2, to_partner),
        )
        self.rest = (
            copy(other, rep, 3, to_partner),
            copy(pick, rep, 4, to_beside),
            copy(pick, partner, 5, to_beside),
        )
        self.rest_arrivals = (
            copy(other, partner, 3, to_partner),
            copy(other, beside, 4, to_beside),
            copy(other, far, 5, to_beside),
        )

    def start(self):
        self.sends[0].start()
        self.sends[1].start()

    def forward(self):
        self.arrivals[1].wait_recv()
        self.sends[2].start()

    def finish(self):
        self.arrivals[0].wait_recv()
        self.arrivals[2].wait_recv()

    def sent(self):
        for send in self.sends:
            send.wait_send()

    def start_rest(self):
        for send in self.rest:
            send.start()

    def finish_rest(self):
        for arrival in self.rest_arrivals:
            arrival.wait_recv()
        for send in self.rest:
            send.wait_send()


class Exchange:
    def __init__(self, shards, rep, own, source, target, span, send_sem, recv_sems):
        self.shards, self.rep, self.own = shards, rep, own
        self.source, self.target, self.span = source, target, span
        self.send_sem, self.recv_sems = send_sem, recv_sems
        self.size = shards // GROUPS

    def start(self):
        size = self.size
        for turn in TURNS:
            group = lax.rem(self.own // size + turn, GROUPS)

            def send(step):
                other = group * size + lax.rem(self.own + step, size)
                remote(
                    self.source(other),
                    self.target(self.own),
                    self.send_sem,
                    self.recv_sems.at[turn],
                    (self.rep, other),
                ).start()

            @pl.loop(0, size // 2 - 1)
            def _(away):
                send(size // 2 + away)
                send(size // 2 - 1 - away)

            send(size - 1)
            if turn:
                send(0)

    def whole(self, first, count, turn):
        span = self.span(first, count)
        return remote(span, span, self.send_sem, self.recv_sems.at[turn], (self.rep, self.own))

    def arrive(self, turn):
        first = lax.rem(self.own // self.size + GROUPS - turn, GROUPS) * self.size
        self.whole(first, self.size if turn else self.size - 1, turn).wait_recv()
        return first

    def finish(self):
        self.whole(0, self.shards - 1, 0).wait_send()


def gather_groups(ring_type, exchange, out, kept, ring_sends, ring_recvs):
    rings = []
    for index, turn in enumerate(TURNS):
        first = exchange.arrive(turn)
        if turn == 0:
            kept.wait()
        ring = ring_type(
            out, first, exchange.size, exchange.rep, exchange.own, ring_sends.at[index], ring_recvs.at[index]
        )
        ring.start()
        if rings:
            rings[-1].forward()
        rings.append(ring)
    rings[-1].forward()
    for ring in rings:
        ring.finish()

    def sent():
        exchange.finish()
        for ring in rings:
            ring.sent()

    return sent


def product(left, right):
    return jnp.dot(left.astype(BF16), right.astype(BF16), preferred_element_type=F32)


def gradient(slots_ref, slot):
    count, shards, rows, quarter = slots_ref.shape[1:]
    return jnp.concatenate(
        [
            slots_ref[slot, index].astype(F32).reshape(shards * rows, quarter).astype(BF16)
            for index in range(count)
        ],
        axis=1,
    )


def outer(grad, side):
    axis = 1 - side
    return lax.dot_general(grad, grad, (((axis,), (axis,)), ((), ())), preferred_element_type=F32)


def step_kernel(
    shards,
    slot_ref,
    grad_ref,
    accum_ref,
    vocab_ref,
    left_ref,
    right_ref,
    slots_out,
    grad_out,
    vocab_out,
    rows_out,
    slot_own,
    grad_own,
    grad_terms,
    grad_relay,
    grad_sum,
    accum_own,
    vocab_own,
    vocab_terms,
    vocab_sum,
    placement,
    outgoing,
    slots,
    graft_part,
    graft_parts,
    graft_totals,
    stats,
    scaled,
    result,
    mine,
    local_sems,
    grad_sends,
    grad_recvs,
    term_sends,
    term_recvs,
    slot_sends,
    slot_recvs,
    part_sends,
    part_recvs,
    row_sends,
    row_recvs,
    slot_ring_sends,
    slot_ring_recvs,
    row_ring_sends,
    row_ring_recvs,
    sum_ring_sends,
    sum_ring_recvs,
    slot_rest_sems,
):
    rep, own = lax.axis_index("rep"), lax.axis_index("fsdp")
    right, left, far = (lax.rem(rep + step, REP) for step in (1, REP - 1, 2))
    to_right, to_left = (right, own), (left, own)
    pick, half = rep // 2, lax.rem(rep, 2)
    blocks, rows, quarter = grad_own.shape
    vocab_quarter = vocab_own.shape[-1]
    order = stats.shape[-1]

    def grad_columns(index):
        return pl.ds(pl.multiple_of(index * quarter, 128), quarter)

    def vocab_columns(index):
        return pl.ds(pl.multiple_of(index * vocab_quarter, 128), vocab_quarter)

    loads = (
        pltpu.make_async_copy(grad_ref.at[:, :, grad_columns(rep)], grad_own, local_sems.at[0]),
        pltpu.make_async_copy(accum_ref.at[:, :, grad_columns(rep)], accum_own, local_sems.at[1]),
        pltpu.make_async_copy(vocab_ref.at[:, :, vocab_columns(rep)], vocab_own, local_sems.at[2]),
        pltpu.make_async_copy(left_ref.at[pick], stats.at[0], local_sems.at[3]),
        pltpu.make_async_copy(right_ref.at[pick], stats.at[1], local_sems.at[4]),
    )
    load_slot = pltpu.make_async_copy(slot_ref, slot_own, local_sems.at[10])
    load_slot.start()
    entered = enter(rep, own, shards)
    for load in loads:
        load.start()

    total_rows = blocks * rows
    spread = jnp.where(
        lax.broadcasted_iota(jnp.int32, (blocks, total_rows), 0)
        == lax.broadcasted_iota(jnp.int32, (blocks, total_rows), 1) // rows,
        1.0,
        0.0,
    )
    load_slot.wait()
    slot_of = jnp.broadcast_to(slot_own[...], (8, blocks)).astype(F32)
    slot_of = product(slot_of, spread)[:1].astype(jnp.int32)
    key = slot_of * rows + lax.rem(lax.broadcasted_iota(jnp.int32, (1, total_rows), 1), rows)
    key = jnp.broadcast_to(key, (shards * rows, total_rows))
    row = lax.broadcasted_iota(jnp.int32, (shards * rows, total_rows), 0)
    place = (row // rows) * (2 * rows) + lax.rem(row, rows)
    for slot in range(2):
        placement[slot] = jnp.where(key == place + slot * rows, 1.0, 0.0).astype(BF16)

    entered()
    front, back = pl.ds(0, blocks // 2), pl.ds(blocks // 2, blocks // 2)
    grad_pairs = (
        (grad_ref.at[front, :, grad_columns(far)], grad_relay.at[0], to_right),
        (grad_ref.at[back, :, grad_columns(far)], grad_relay.at[1], to_left),
        (grad_ref.at[:, :, grad_columns(right)], grad_terms.at[0], to_right),
        (grad_ref.at[:, :, grad_columns(left)], grad_terms.at[1], to_left),
        (grad_relay.at[0], grad_terms.at[2, front], to_right),
        (grad_relay.at[1], grad_terms.at[2, back], to_left),
    )
    grad_copies = [
        remote(source, target, grad_sends.at[index], grad_recvs.at[index], device)
        for index, (source, target, device) in enumerate(grad_pairs)
    ]
    for copy in grad_copies[:4]:
        copy.start()
    vocab_copies = []
    for step in range(1, REP):
        other = lax.rem(rep + step, REP)
        vocab_copies.append(
            remote(
                vocab_ref.at[:, :, vocab_columns(other)],
                vocab_terms.at[step - 1],
                term_sends.at[step - 1],
                term_recvs.at[step - 1],
                (other, own),
            )
        )
    for index in range(2):
        grad_copies[index].wait_recv()
        grad_copies[4 + index].start()
    loads[0].wait()
    for copy in grad_copies[2:]:
        copy.wait_recv()
    total = grad_own[...].astype(F32)
    for step in range(REP - 1):
        total = total + grad_terms[step].astype(F32)
    flat = total.reshape(total_rows, quarter).astype(BF16)
    for slot in range(2):
        placed = jnp.dot(placement[slot], flat, preferred_element_type=F32)
        outgoing[:, slot] = placed.reshape(shards, rows, quarter).astype(BF16)
    slot_exchange = Exchange(
        shards,
        rep,
        own,
        lambda other: outgoing.at[other],
        lambda source: slots.at[:, rep, source],
        lambda first, count: slots.at[:, rep, pl.ds(first, count)],
        slot_sends,
        slot_recvs,
    )
    slot_exchange.start()
    keep = pltpu.make_async_copy(outgoing.at[own], slots.at[:, rep, own], local_sems.at[5])
    keep.start()
    for copy in vocab_copies:
        copy.start()
    grad_sum[...] = total.astype(BF16)
    keep_sum = pltpu.make_async_copy(grad_sum, grad_out.at[rep], local_sems.at[6])
    keep_sum.start()

    loads[1].wait()
    value = flat.astype(F32)
    accum_new = accum_own[...].reshape(total_rows, quarter) + value * value
    grafted = value / (jnp.sqrt(accum_new) + 1e-10)
    slot_count = 2 * shards
    slot = lax.broadcasted_iota(jnp.int32, (slot_count, total_rows), 0)
    chosen = jnp.where(jnp.broadcast_to(slot_of, (slot_count, total_rows)) == slot, 1.0, 0.0)
    by_slot = jnp.dot(chosen, grafted * grafted, precision=lax.Precision.HIGHEST)
    ones = jnp.ones((8, quarter), F32)
    parts = lax.dot_general(
        ones, by_slot, (((1,), (1,)), ((), ())), precision=lax.Precision.HIGHEST
    )
    graft_part[...] = parts[:1]
    graft_parts[pl.ds(own, 1)] = parts[:1][None]
    part_exchange = Exchange(
        shards,
        rep,
        own,
        lambda other: graft_part,
        lambda source: graft_parts.at[source],
        lambda first, count: graft_parts.at[pl.ds(first, count)],
        part_sends,
        part_recvs,
    )
    part_exchange.start()

    slots_sent = gather_groups(PairGather, slot_exchange, slots, keep, slot_ring_sends, slot_ring_recvs)
    slot_rest = PairGather(slots, 0, shards, rep, own, slot_rest_sems.at[0], slot_rest_sems.at[1])
    slot_rest.start_rest()
    keep_sum.wait()
    grad_ring = RingGather(grad_out, 0, blocks, rep, own, sum_ring_sends.at[0], sum_ring_recvs.at[0])
    grad_ring.start()
    keep_vocab = pltpu.make_async_copy(vocab_sum, vocab_out.at[rep], local_sems.at[8])
    vocab_ring = RingGather(
        vocab_out, 0, vocab_own.shape[0], rep, own, sum_ring_sends.at[1], sum_ring_recvs.at[1]
    )
    total_copies = []
    for step in range(1, REP):
        other, source = lax.rem(rep + step, REP), lax.rem(rep + REP - step, REP)
        index = REP - 1 + step - 1
        pieces = [graft_totals.at[pl.ds(place, 1)] for place in (rep, source)]
        total_copies.append(
            [remote(piece, piece, term_sends.at[index], term_recvs.at[index], (other, own)) for piece in pieces]
        )

    grad = gradient(slots, pick)
    row = lax.broadcasted_iota(jnp.int32, (order, order), 0)
    column = lax.broadcasted_iota(jnp.int32, (order, order), 1)
    for side in range(2):
        loads[3 + side].wait()
        matrix = stats[side] + outer(grad, side)
        start = matrix * (1.0 / jnp.sqrt(jnp.full((1, 1), jnp.sum(matrix * matrix), F32)))
        scaled[side] = start
        result[side] = jnp.where(row == column, 1.25, 0.0) - 0.25 * start

    @pl.loop(1, ITERS)
    def _(iteration):
        for side in range(2):
            value = scaled[side]
            excess = product(value, value) * 0.0625 - 0.625 * value
            change = product(excess, excess) + 3.125 * excess
            value = product(change, value) + 2.44140625 * value
            scaled[side] = value
            root = result[side]
            result[side] = 1.25 * root - 0.25 * product(root, value)

        @pl.when(iteration == 3)
        def _():
            for turn in TURNS:
                part_exchange.arrive(turn)
            graft_totals[pl.ds(rep, 1)] = jnp.sum(graft_parts[...], axis=0)[None]
            for copy, arrival in total_copies:
                copy.start()
            loads[2].wait()
            for copy in vocab_copies:
                copy.wait_recv()
            vocab_total = vocab_own[...].astype(F32)
            for step in range(REP - 1):
                vocab_total = vocab_total + vocab_terms[step].astype(F32)
            vocab_sum[...] = vocab_total.astype(BF16)
            keep_vocab.start()

        @pl.when(iteration == 4)
        def _():
            keep_vocab.wait()
            vocab_ring.start()

    shampoo = product(product(result[0], grad), result[1])
    for copy, arrival in total_copies:
        arrival.wait_recv()
    entries = float(order * order)
    lane = lax.broadcasted_iota(jnp.int32, (1, slot_count), 1)
    graft_total = jnp.sum(jnp.where(lane == 2 * own + pick, jnp.sum(graft_totals[...], axis=0), 0.0))
    graft_mean = jnp.full((1, 1), graft_total / entries, F32)
    shampoo_mean = jnp.full((1, 1), jnp.sum(shampoo * shampoo) / entries, F32)
    scale = jnp.sqrt(graft_mean) / jnp.sqrt(shampoo_mean + 1e-06)
    direction = shampoo * scale
    direction = jnp.where(half == 0, direction[:, : order // 2], direction[:, order // 2 :])
    mine[...] = direction.reshape(mine.shape).astype(BF16)
    row_exchange = Exchange(
        shards,
        rep,
        own,
        lambda other: mine.at[other],
        lambda source: rows_out.at[rep, source],
        lambda first, count: rows_out.at[rep, pl.ds(first, count)],
        row_sends,
        row_recvs,
    )
    row_exchange.start()
    keep_rows = pltpu.make_async_copy(mine.at[own], rows_out.at[rep, own], local_sems.at[9])
    keep_rows.start()
    grad_ring.forward()
    vocab_ring.forward()
    slot_rest.finish_rest()
    keep_slots = pltpu.make_async_copy(slots, slots_out, local_sems.at[7])
    keep_slots.start()
    rows_sent = gather_groups(RingGather, row_exchange, rows_out, keep_rows, row_ring_sends, row_ring_recvs)

    grad_ring.finish()
    vocab_ring.finish()
    keep_slots.wait()
    for copy in grad_copies + vocab_copies:
        copy.wait_send()
    for copy, arrival in total_copies:
        copy.wait_send()
    part_exchange.finish()
    grad_ring.sent()
    vocab_ring.sent()
    slots_sent()
    rows_sent()


def shampoo_step(block_slot, grads, accum, vocab, left, right):
    shards = lax.axis_size("fsdp")
    blocks, rows, order = grads.shape
    quarter = order // REP
    vocab_shape = vocab.shape[:2] + (vocab.shape[-1] // REP,)
    row_shape = (REP, shards, rows, order // 2)
    slot_shape = (2, REP, shards, rows, quarter)
    dma = pltpu.SemaphoreType.DMA
    return pl.pallas_call(
        functools.partial(step_kernel, shards),
        out_shape=(
            jax.ShapeDtypeStruct(slot_shape, BF16),
            jax.ShapeDtypeStruct((REP, blocks, rows, quarter), BF16),
            jax.ShapeDtypeStruct((REP,) + vocab_shape, BF16),
            jax.ShapeDtypeStruct(row_shape, BF16),
        ),
        in_specs=[HBM] * 6,
        out_specs=(ANY, ANY, ANY, ANY),
        scratch_shapes=[
            pltpu.VMEM((1, blocks), jnp.int32),
            pltpu.VMEM((blocks, rows, quarter), BF16),
            pltpu.VMEM((REP - 1, blocks, rows, quarter), BF16),
            pltpu.VMEM((2, blocks // 2, rows, quarter), BF16),
            pltpu.VMEM((blocks, rows, quarter), BF16),
            pltpu.VMEM((blocks, rows, quarter), F32),
            pltpu.VMEM(vocab_shape, BF16),
            pltpu.VMEM((REP - 1,) + vocab_shape, BF16),
            pltpu.VMEM(vocab_shape, BF16),
            pltpu.VMEM((2, shards * rows, blocks * rows), BF16),
            pltpu.VMEM((shards, 2, rows, quarter), BF16),
            pltpu.VMEM(slot_shape, BF16),
            pltpu.VMEM((1, 2 * shards), F32),
            pltpu.VMEM((shards, 1, 2 * shards), F32),
            pltpu.VMEM((REP, 1, 2 * shards), F32),
            pltpu.VMEM((2, order, order), F32),
            pltpu.VMEM((2, order, order), F32),
            pltpu.VMEM((2, order, order), F32),
            pltpu.VMEM(row_shape[1:], BF16),
            dma((11,)),
            dma((6,)),
            dma((6,)),
            dma((2 * (REP - 1),)),
            dma((2 * (REP - 1),)),
            dma,
            dma((GROUPS,)),
            dma,
            dma((GROUPS,)),
            dma,
            dma((GROUPS,)),
            dma((GROUPS, 6)),
            dma((GROUPS, 6)),
            dma((GROUPS, 4)),
            dma((GROUPS, 4)),
            dma((2, 4)),
            dma((2, 4)),
            dma((2, 6)),
        ],
        compiler_params=pltpu.CompilerParams(
            collective_id=0, has_side_effects=True, vmem_limit_bytes=30 * 1024 * 1024
        ),
        name="shampoo_step",
    )(
        *(
            pltpu.with_memory_space_constraint(array, pltpu.HBM)
            for array in (block_slot.reshape(1, -1), grads, accum, vocab, left, right)
        )
    )


def finish_kernel(
    slot_ref,
    slots_ref,
    grad_ref,
    vocab_ref,
    rows_ref,
    accum_ref,
    left_ref,
    right_ref,
    vocab_accum_ref,
    direction_out,
    accum_out,
    left_out,
    right_out,
    vocab_out,
    step_out,
    direction,
    accum,
    stats,
    vocab_accum,
    vocab_step,
    sems,
):
    half = rows_ref.shape[-1]
    stores = []

    def store(source, target):
        stores.append(pltpu.make_async_copy(source, target, sems.at[len(stores)]))
        stores[-1].start()

    for slot in range(2):
        grad = gradient(slots_ref, slot)
        for side, (ref, out) in enumerate(((left_ref, left_out), (right_ref, right_out))):
            stats[side, slot] = ref[slot] + outer(grad, side)
            store(stats.at[side, slot], out.at[slot])
    for index in range(REP):
        quarter = grad_ref.shape[-1]
        columns = slice(index * quarter, (index + 1) * quarter)
        grad = grad_ref[index].astype(F32)
        accum[:, :, columns] = accum_ref[:, :, columns] + grad * grad
    store(accum, accum_out)
    for index in range(REP):
        quarter = vocab_ref.shape[-1]
        columns = slice(index * quarter, (index + 1) * quarter)
        vocab = vocab_ref[index].astype(F32)
        value = vocab_accum_ref[:, :, columns] + vocab * vocab
        vocab_accum[:, :, columns] = value
        vocab_step[:, :, columns] = (vocab / (jnp.sqrt(value) + 1e-10)).astype(BF16)
    store(vocab_accum, vocab_out)
    store(vocab_step, step_out)

    @pl.loop(0, direction.shape[0], unroll=4)
    def _(block):
        slot = slot_ref[block]
        owner, pick = slot // 2, lax.rem(slot, 2)
        for side in range(2):
            direction[block, :, side * half : (side + 1) * half] = rows_ref[2 * pick + side, owner]

    store(direction, direction_out)
    for copy in stores:
        copy.wait()


def finish(block_slot, slots, grads, vocab, rows, accum, left, right, vocab_accum):
    direction = (block_slot.shape[0], rows.shape[2], 2 * rows.shape[3])
    return pl.pallas_call(
        finish_kernel,
        out_shape=(
            jax.ShapeDtypeStruct(direction, BF16),
            jax.ShapeDtypeStruct(accum.shape, F32),
            jax.ShapeDtypeStruct(left.shape, F32),
            jax.ShapeDtypeStruct(right.shape, F32),
            jax.ShapeDtypeStruct(vocab_accum.shape, F32),
            jax.ShapeDtypeStruct(vocab_accum.shape, BF16),
        ),
        in_specs=[SMEM] + [VMEM] * 8,
        out_specs=(HBM,) * 6,
        scratch_shapes=[
            pltpu.VMEM(direction, BF16),
            pltpu.VMEM(accum.shape, F32),
            pltpu.VMEM((2,) + left.shape, F32),
            pltpu.VMEM(vocab_accum.shape, F32),
            pltpu.VMEM(vocab_accum.shape, BF16),
            pltpu.SemaphoreType.DMA((8,)),
        ],
        compiler_params=pltpu.CompilerParams(vmem_limit_bytes=30 * 1024 * 1024),
        name="finish",
    )(block_slot, slots, grads, vocab, rows, accum, left, right, vocab_accum)


def on_device(
    grad_blocks, graft_accum, left_stats, right_stats, block_slot, vocab_grads, vocab_accum
):
    slots, grads, vocab, rows = shampoo_step(
        block_slot, grad_blocks[0], graft_accum, vocab_grads[0], left_stats, right_stats
    )
    return finish(
        block_slot, slots, grads, vocab, rows, graft_accum, left_stats, right_stats, vocab_accum
    )


def solution(mesh):
    in_specs = (
        P("rep", None, "fsdp", None),
        P(None, "fsdp", None),
        P("fsdp", None, None),
        P("fsdp", None, None),
        P(),
        P("rep", None, "fsdp", None),
        P(None, "fsdp", None),
    )
    out_specs = (
        P(None, "fsdp", None),
        P(None, "fsdp", None),
        P("fsdp", None, None),
        P("fsdp", None, None),
        P(None, "fsdp", None),
        P(None, "fsdp", None),
    )
    return jax.shard_map(
        on_device, mesh=mesh, in_specs=in_specs, out_specs=out_specs, check_vma=False
    )
```

```python
import functools

import jax
import jax.numpy as jnp
from jax import lax
from jax.experimental import pallas as pl
from jax.experimental.pallas import tpu as pltpu
from jax.sharding import PartitionSpec as P

ITERS = 6
REP = 4
GROUPS = 4
TURNS = (0, 1, 3, 2)
MESH = pl.DeviceIdType.MESH
F32 = jnp.float32
BF16 = jnp.bfloat16
ANY = pl.BlockSpec(memory_space=pl.ANY)
HBM = pl.BlockSpec(memory_space=pltpu.HBM)
VMEM = pl.BlockSpec(memory_space=pltpu.VMEM)
SMEM = pl.BlockSpec(memory_space=pltpu.SMEM)


def remote(src, dst, send_sem, recv_sem, device):
    return pltpu.make_async_remote_copy(
        src_ref=src,
        dst_ref=dst,
        send_sem=send_sem,
        recv_sem=recv_sem,
        device_id=device,
        device_id_type=MESH,
    )


def enter(rep, own, shards):
    barrier = pltpu.get_barrier_semaphore()

    size = shards // GROUPS
    for turn in (2, 1, 3, 0):
        group = lax.rem(own // size + turn, GROUPS)

        @pl.loop(1 if turn == 0 else 0, size)
        def _(step):
            other = group * size + lax.rem(own + step, size)
            pl.semaphore_signal(barrier, inc=1, device_id=(rep, other), device_id_type=MESH)

    for step in range(1, REP):
        other = lax.rem(rep + step, REP)
        pl.semaphore_signal(barrier, inc=1, device_id=(other, own), device_id_type=MESH)
    return lambda: pl.semaphore_wait(barrier, shards - 1 + REP - 1)


class RingGather:
    def __init__(self, out, first, count, rep, own, send_sems, recv_sems):
        self.send_sems, self.recv_sems = send_sems, recv_sems
        right, left = lax.rem(rep + 1, REP), lax.rem(rep + REP - 1, REP)
        far = lax.rem(rep + 2, REP)
        half = count // 2
        whole, front, back = pl.ds(first, count), pl.ds(first, half), pl.ds(first + half, half)
        to_right, to_left = (right, own), (left, own)
        self.sends = (
            self.copy(out.at[rep, whole], 0, to_right),
            self.copy(out.at[rep, whole], 1, to_left),
            self.copy(out.at[left, front], 2, to_right),
            self.copy(out.at[right, back], 3, to_left),
        )
        self.arrivals = (
            self.copy(out.at[left, whole], 0, to_right),
            self.copy(out.at[right, whole], 1, to_left),
            self.copy(out.at[far, front], 2, to_right),
            self.copy(out.at[far, back], 3, to_left),
        )

    def copy(self, piece, index, device):
        return remote(piece, piece, self.send_sems.at[index], self.recv_sems.at[index], device)

    def start(self):
        self.sends[0].start()
        self.sends[1].start()

    def forward(self):
        self.arrivals[0].wait_recv()
        self.sends[2].start()
        self.arrivals[1].wait_recv()
        self.sends[3].start()

    def finish(self):
        self.arrivals[2].wait_recv()
        self.arrivals[3].wait_recv()

    def sent(self):
        for send in self.sends:
            send.wait_send()


class PairGather:
    def __init__(self, slots, first, count, rep, own, send_sems, recv_sems):
        self.send_sems, self.recv_sems = send_sems, recv_sems
        odd = lax.rem(rep, 2)
        partner, beside = rep + 1 - 2 * odd, lax.rem(rep + 3 + 2 * odd, REP)
        far = lax.rem(rep + 2, REP)
        pick, rows = rep // 2, pl.ds(first, count)
        other = 1 - pick
        to_partner, to_beside = (partner, own), (beside, own)

        def copy(slot, index, sem, device):
            piece = slots.at[slot, index, rows]
            return remote(piece, piece, send_sems.at[sem], recv_sems.at[sem], device)

        self.sends = (
            copy(pick, rep, 0, to_partner),
            copy(other, rep, 1, to_beside),
            copy(pick, beside, 2, to_partner),
        )
        self.arrivals = (
            copy(pick, partner, 0, to_partner),
            copy(pick, beside, 1, to_beside),
            copy(pick, far, 2, to_partner),
        )
        self.rest = (
            copy(other, rep, 3, to_partner),
            copy(pick, rep, 4, to_beside),
            copy(pick, partner, 5, to_beside),
        )
        self.rest_arrivals = (
            copy(other, partner, 3, to_partner),
            copy(other, beside, 4, to_beside),
            copy(other, far, 5, to_beside),
        )

    def start(self):
        self.sends[0].start()
        self.sends[1].start()

    def forward(self):
        self.arrivals[1].wait_recv()
        self.sends[2].start()

    def finish(self):
        self.arrivals[0].wait_recv()
        self.arrivals[2].wait_recv()

    def sent(self):
        for send in self.sends:
            send.wait_send()

    def start_rest(self):
        for send in self.rest:
            send.start()

    def finish_rest(self):
        for arrival in self.rest_arrivals:
            arrival.wait_recv()
        for send in self.rest:
            send.wait_send()


class Exchange:
    def __init__(self, shards, rep, own, source, target, span, send_sem, recv_sems):
        self.shards, self.rep, self.own = shards, rep, own
        self.source, self.target, self.span = source, target, span
        self.send_sem, self.recv_sems = send_sem, recv_sems
        self.size = shards // GROUPS

    def start(self):
        size = self.size
        for turn in TURNS:
            group = lax.rem(self.own // size + turn, GROUPS)

            def send(step):
                other = group * size + lax.rem(self.own + step, size)
                remote(
                    self.source(other),
                    self.target(self.own),
                    self.send_sem,
                    self.recv_sems.at[turn],
                    (self.rep, other),
                ).start()

            @pl.loop(0, size // 2 - 1)
            def _(away):
                send(size // 2 + away)
                send(size // 2 - 1 - away)

            send(size - 1)
            if turn:
                send(0)

    def whole(self, first, count, turn):
        span = self.span(first, count)
        return remote(span, span, self.send_sem, self.recv_sems.at[turn], (self.rep, self.own))

    def arrive(self, turn):
        first = lax.rem(self.own // self.size + GROUPS - turn, GROUPS) * self.size
        self.whole(first, self.size if turn else self.size - 1, turn).wait_recv()
        return first

    def finish(self):
        self.whole(0, self.shards - 1, 0).wait_send()


def gather_groups(ring_type, exchange, out, kept, ring_sends, ring_recvs):
    rings = []
    for index, turn in enumerate(TURNS):
        first = exchange.arrive(turn)
        if turn == 0:
            kept.wait()
        ring = ring_type(
            out, first, exchange.size, exchange.rep, exchange.own, ring_sends.at[index], ring_recvs.at[index]
        )
        ring.start()
        if rings:
            rings[-1].forward()
        rings.append(ring)
    rings[-1].forward()
    for ring in rings:
        ring.finish()

    def sent():
        exchange.finish()
        for ring in rings:
            ring.sent()

    return sent


def product(left, right):
    return jnp.dot(left, right, preferred_element_type=F32)


def symmetric_product(left, right, side):
    half = left.shape[-1] // 2
    return product(left[side, :half], right[side, :, :half]), product(left[side], right[side, :, half:])


def parts_of(matrix, side):
    half = matrix.shape[-1] // 2
    return matrix[side, :half, :half], matrix[side, :, half:]


def put_parts(matrix, side, parts):
    half = matrix.shape[-1] // 2
    matrix[side, :half, :half] = parts[0]
    matrix[side, :, half:] = parts[1]


def put_operand(matrix, side, parts):
    half = matrix.shape[-1] // 2
    corner, right = (part.astype(BF16) for part in parts)
    put_parts(matrix, side, (corner, right))
    matrix[side, half:, :half] = right[:half].T


def combine(parts, factor, others, other_factor):
    return tuple(part * factor + other * other_factor for part, other in zip(parts, others))


def gradient(slots_ref, slot):
    count, shards, rows, quarter = slots_ref.shape[1:]
    return jnp.concatenate(
        [
            slots_ref[slot, index].astype(F32).reshape(shards * rows, quarter).astype(BF16)
            for index in range(count)
        ],
        axis=1,
    )


def outer(grad, side):
    axis = 1 - side
    return lax.dot_general(grad, grad, (((axis,), (axis,)), ((), ())), preferred_element_type=F32)


def step_kernel(
    shards,
    slot_ref,
    grad_ref,
    accum_ref,
    vocab_ref,
    left_ref,
    right_ref,
    slots_out,
    grad_out,
    vocab_out,
    rows_out,
    slot_own,
    grad_own,
    grad_terms,
    grad_relay,
    grad_sum,
    accum_own,
    vocab_own,
    vocab_terms,
    vocab_sum,
    placement,
    outgoing,
    slots,
    graft_part,
    graft_parts,
    graft_totals,
    stats,
    scaled,
    result,
    scaled_operand,
    excess_operand,
    change_operand,
    result_operand,
    mine,
    local_sems,
    grad_sends,
    grad_recvs,
    term_sends,
    term_recvs,
    slot_sends,
    slot_recvs,
    part_sends,
    part_recvs,
    row_sends,
    row_recvs,
    slot_ring_sends,
    slot_ring_recvs,
    row_ring_sends,
    row_ring_recvs,
    sum_ring_sends,
    sum_ring_recvs,
    slot_rest_sems,
):
    rep, own = lax.axis_index("rep"), lax.axis_index("fsdp")
    right, left, far = (lax.rem(rep + step, REP) for step in (1, REP - 1, 2))
    to_right, to_left = (right, own), (left, own)
    pick, half = rep // 2, lax.rem(rep, 2)
    blocks, rows, quarter = grad_own.shape
    vocab_quarter = vocab_own.shape[-1]
    order = stats.shape[-1]

    def grad_columns(index):
        return pl.ds(pl.multiple_of(index * quarter, 128), quarter)

    def vocab_columns(index):
        return pl.ds(pl.multiple_of(index * vocab_quarter, 128), vocab_quarter)

    loads = (
        pltpu.make_async_copy(grad_ref.at[:, :, grad_columns(rep)], grad_own, local_sems.at[0]),
        pltpu.make_async_copy(accum_ref.at[:, :, grad_columns(rep)], accum_own, local_sems.at[1]),
        pltpu.make_async_copy(vocab_ref.at[:, :, vocab_columns(rep)], vocab_own, local_sems.at[2]),
        pltpu.make_async_copy(left_ref.at[pick], stats.at[0], local_sems.at[3]),
        pltpu.make_async_copy(right_ref.at[pick], stats.at[1], local_sems.at[4]),
    )
    load_slot = pltpu.make_async_copy(slot_ref, slot_own, local_sems.at[10])
    load_slot.start()
    entered = enter(rep, own, shards)
    for load in loads:
        load.start()

    total_rows = blocks * rows
    spread = jnp.where(
        lax.broadcasted_iota(jnp.int32, (blocks, total_rows), 0)
        == lax.broadcasted_iota(jnp.int32, (blocks, total_rows), 1) // rows,
        1.0,
        0.0,
    )
    load_slot.wait()
    slot_of = jnp.broadcast_to(slot_own[...], (8, blocks)).astype(F32)
    slot_of = product(slot_of.astype(BF16), spread.astype(BF16))[:1].astype(jnp.int32)
    key = slot_of * rows + lax.rem(lax.broadcasted_iota(jnp.int32, (1, total_rows), 1), rows)
    key = jnp.broadcast_to(key, (shards * rows, total_rows))
    row = lax.broadcasted_iota(jnp.int32, (shards * rows, total_rows), 0)
    place = (row // rows) * (2 * rows) + lax.rem(row, rows)
    for slot in range(2):
        placement[slot] = jnp.where(key == place + slot * rows, 1.0, 0.0).astype(BF16)

    entered()
    front, back = pl.ds(0, blocks // 2), pl.ds(blocks // 2, blocks // 2)
    grad_pairs = (
        (grad_ref.at[front, :, grad_columns(far)], grad_relay.at[0], to_right),
        (grad_ref.at[back, :, grad_columns(far)], grad_relay.at[1], to_left),
        (grad_ref.at[:, :, grad_columns(right)], grad_terms.at[0], to_right),
        (grad_ref.at[:, :, grad_columns(left)], grad_terms.at[1], to_left),
        (grad_relay.at[0], grad_terms.at[2, front], to_right),
        (grad_relay.at[1], grad_terms.at[2, back], to_left),
    )
    grad_copies = [
        remote(source, target, grad_sends.at[index], grad_recvs.at[index], device)
        for index, (source, target, device) in enumerate(grad_pairs)
    ]
    for copy in grad_copies[:4]:
        copy.start()
    vocab_copies = []
    for step in range(1, REP):
        other = lax.rem(rep + step, REP)
        vocab_copies.append(
            remote(
                vocab_ref.at[:, :, vocab_columns(other)],
                vocab_terms.at[step - 1],
                term_sends.at[step - 1],
                term_recvs.at[step - 1],
                (other, own),
            )
        )
    for index in range(2):
        grad_copies[index].wait_recv()
        grad_copies[4 + index].start()
    loads[0].wait()
    for copy in grad_copies[2:]:
        copy.wait_recv()
    total = grad_own[...].astype(F32)
    for step in range(REP - 1):
        total = total + grad_terms[step].astype(F32)
    flat = total.reshape(total_rows, quarter).astype(BF16)
    for slot in range(2):
        placed = jnp.dot(placement[slot], flat, preferred_element_type=F32)
        outgoing[:, slot] = placed.reshape(shards, rows, quarter).astype(BF16)
    slot_exchange = Exchange(
        shards,
        rep,
        own,
        lambda other: outgoing.at[other],
        lambda source: slots.at[:, rep, source],
        lambda first, count: slots.at[:, rep, pl.ds(first, count)],
        slot_sends,
        slot_recvs,
    )
    slot_exchange.start()
    keep = pltpu.make_async_copy(outgoing.at[own], slots.at[:, rep, own], local_sems.at[5])
    keep.start()
    for copy in vocab_copies:
        copy.start()
    grad_sum[...] = total.astype(BF16)
    keep_sum = pltpu.make_async_copy(grad_sum, grad_out.at[rep], local_sems.at[6])
    keep_sum.start()

    loads[1].wait()
    value = flat.astype(F32)
    accum_new = accum_own[...].reshape(total_rows, quarter) + value * value
    grafted = value / (jnp.sqrt(accum_new) + 1e-10)
    slot_count = 2 * shards
    slot = lax.broadcasted_iota(jnp.int32, (slot_count, total_rows), 0)
    chosen = jnp.where(jnp.broadcast_to(slot_of, (slot_count, total_rows)) == slot, 1.0, 0.0)
    by_slot = jnp.dot(chosen, grafted * grafted, precision=lax.Precision.HIGHEST)
    ones = jnp.ones((8, quarter), F32)
    parts = lax.dot_general(
        ones, by_slot, (((1,), (1,)), ((), ())), precision=lax.Precision.HIGHEST
    )
    graft_part[...] = parts[:1]
    graft_parts[pl.ds(own, 1)] = parts[:1][None]
    part_exchange = Exchange(
        shards,
        rep,
        own,
        lambda other: graft_part,
        lambda source: graft_parts.at[source],
        lambda first, count: graft_parts.at[pl.ds(first, count)],
        part_sends,
        part_recvs,
    )
    part_exchange.start()

    slots_sent = gather_groups(PairGather, slot_exchange, slots, keep, slot_ring_sends, slot_ring_recvs)
    slot_rest = PairGather(slots, 0, shards, rep, own, slot_rest_sems.at[0], slot_rest_sems.at[1])
    slot_rest.start_rest()
    keep_sum.wait()
    grad_ring = RingGather(grad_out, 0, blocks, rep, own, sum_ring_sends.at[0], sum_ring_recvs.at[0])
    grad_ring.start()
    keep_vocab = pltpu.make_async_copy(vocab_sum, vocab_out.at[rep], local_sems.at[8])
    vocab_ring = RingGather(
        vocab_out, 0, vocab_own.shape[0], rep, own, sum_ring_sends.at[1], sum_ring_recvs.at[1]
    )
    total_copies = []
    for step in range(1, REP):
        other, source = lax.rem(rep + step, REP), lax.rem(rep + REP - step, REP)
        index = REP - 1 + step - 1
        pieces = [graft_totals.at[pl.ds(place, 1)] for place in (rep, source)]
        total_copies.append(
            [remote(piece, piece, term_sends.at[index], term_recvs.at[index], (other, own)) for piece in pieces]
        )

    grad = gradient(slots, pick)
    middle = order // 2
    row = lax.broadcasted_iota(jnp.int32, (order, order), 0)
    column = lax.broadcasted_iota(jnp.int32, (order, order), 1)
    identity = jnp.where(row == column, 1.25, 0.0)
    identity = (identity[:middle, :middle], identity[:, middle:])
    starts = []
    for side in range(2):
        loads[3 + side].wait()
        start = []
        for part, lines, columns in zip(
            parts_of(stats, side), (slice(0, middle), slice(None)), (slice(0, middle), slice(middle, None))
        ):
            if side == 0:
                pair, dims = (grad[lines], grad[columns]), (((1,), (1,)), ((), ()))
            else:
                pair, dims = (grad[:, lines], grad[:, columns]), (((0,), (0,)), ((), ()))
            start.append(part + lax.dot_general(*pair, dims, preferred_element_type=F32))
        starts.append(start)
    for side in range(2):
        corner, right_half = starts[side]
        squares = jnp.sum(corner * corner) + jnp.sum(right_half * right_half)
        squares = squares + jnp.sum(right_half[:middle] * right_half[:middle])
        inverse = 1.0 / jnp.sqrt(jnp.full((1, 1), squares, F32))
        value = (corner * inverse, right_half * inverse)
        put_parts(scaled, side, value)
        put_operand(scaled_operand, side, value)
        root = combine(identity, 1.0, value, -0.25)
        put_parts(result, side, root)
        put_operand(result_operand, side, root)

    @pl.loop(1, ITERS)
    def _(iteration):
        excess = []
        for side in range(2):
            square = symmetric_product(scaled_operand, scaled_operand, side)
            excess.append(combine(square, 0.0625, parts_of(scaled, side), -0.625))
            put_operand(excess_operand, side, excess[side])
        for side in range(2):
            change = symmetric_product(excess_operand, excess_operand, side)
            put_operand(change_operand, side, combine(change, 1.0, excess[side], 3.125))
        for side in range(2):
            value = symmetric_product(change_operand, scaled_operand, side)
            value = combine(value, 1.0, parts_of(scaled, side), 2.44140625)
            put_parts(scaled, side, value)
            put_operand(scaled_operand, side, value)
        for side in range(2):
            root = symmetric_product(result_operand, scaled_operand, side)
            root = combine(root, -0.25, parts_of(result, side), 1.25)
            put_parts(result, side, root)
            put_operand(result_operand, side, root)

        @pl.when(iteration == 3)
        def _():
            for turn in TURNS:
                part_exchange.arrive(turn)
            graft_totals[pl.ds(rep, 1)] = jnp.sum(graft_parts[...], axis=0)[None]
            for copy, arrival in total_copies:
                copy.start()
            loads[2].wait()
            for copy in vocab_copies:
                copy.wait_recv()
            vocab_total = vocab_own[...].astype(F32)
            for step in range(REP - 1):
                vocab_total = vocab_total + vocab_terms[step].astype(F32)
            vocab_sum[...] = vocab_total.astype(BF16)
            keep_vocab.start()

        @pl.when(iteration == 4)
        def _():
            keep_vocab.wait()
            vocab_ring.start()

    shampoo = product(product(result_operand[0], grad).astype(BF16), result_operand[1])
    for copy, arrival in total_copies:
        arrival.wait_recv()
    entries = float(order * order)
    lane = lax.broadcasted_iota(jnp.int32, (1, slot_count), 1)
    graft_total = jnp.sum(jnp.where(lane == 2 * own + pick, jnp.sum(graft_totals[...], axis=0), 0.0))
    graft_mean = jnp.full((1, 1), graft_total / entries, F32)
    shampoo_mean = jnp.full((1, 1), jnp.sum(shampoo * shampoo) / entries, F32)
    scale = jnp.sqrt(graft_mean) / jnp.sqrt(shampoo_mean + 1e-06)
    direction = shampoo * scale
    direction = jnp.where(half == 0, direction[:, : order // 2], direction[:, order // 2 :])
    mine[...] = direction.reshape(mine.shape).astype(BF16)
    row_exchange = Exchange(
        shards,
        rep,
        own,
        lambda other: mine.at[other],
        lambda source: rows_out.at[rep, source],
        lambda first, count: rows_out.at[rep, pl.ds(first, count)],
        row_sends,
        row_recvs,
    )
    row_exchange.start()
    keep_rows = pltpu.make_async_copy(mine.at[own], rows_out.at[rep, own], local_sems.at[9])
    keep_rows.start()
    grad_ring.forward()
    vocab_ring.forward()
    slot_rest.finish_rest()
    keep_slots = pltpu.make_async_copy(slots, slots_out, local_sems.at[7])
    keep_slots.start()
    rows_sent = gather_groups(RingGather, row_exchange, rows_out, keep_rows, row_ring_sends, row_ring_recvs)

    grad_ring.finish()
    vocab_ring.finish()
    keep_slots.wait()
    for copy in grad_copies + vocab_copies:
        copy.wait_send()
    for copy, arrival in total_copies:
        copy.wait_send()
    part_exchange.finish()
    grad_ring.sent()
    vocab_ring.sent()
    slots_sent()
    rows_sent()


def shampoo_step(block_slot, grads, accum, vocab, left, right):
    shards = lax.axis_size("fsdp")
    blocks, rows, order = grads.shape
    quarter = order // REP
    vocab_shape = vocab.shape[:2] + (vocab.shape[-1] // REP,)
    row_shape = (REP, shards, rows, order // 2)
    slot_shape = (2, REP, shards, rows, quarter)
    dma = pltpu.SemaphoreType.DMA
    return pl.pallas_call(
        functools.partial(step_kernel, shards),
        out_shape=(
            jax.ShapeDtypeStruct(slot_shape, BF16),
            jax.ShapeDtypeStruct((REP, blocks, rows, quarter), BF16),
            jax.ShapeDtypeStruct((REP,) + vocab_shape, BF16),
            jax.ShapeDtypeStruct(row_shape, BF16),
        ),
        in_specs=[HBM] * 6,
        out_specs=(ANY, ANY, ANY, ANY),
        scratch_shapes=[
            pltpu.VMEM((1, blocks), jnp.int32),
            pltpu.VMEM((blocks, rows, quarter), BF16),
            pltpu.VMEM((REP - 1, blocks, rows, quarter), BF16),
            pltpu.VMEM((2, blocks // 2, rows, quarter), BF16),
            pltpu.VMEM((blocks, rows, quarter), BF16),
            pltpu.VMEM((blocks, rows, quarter), F32),
            pltpu.VMEM(vocab_shape, BF16),
            pltpu.VMEM((REP - 1,) + vocab_shape, BF16),
            pltpu.VMEM(vocab_shape, BF16),
            pltpu.VMEM((2, shards * rows, blocks * rows), BF16),
            pltpu.VMEM((shards, 2, rows, quarter), BF16),
            pltpu.VMEM(slot_shape, BF16),
            pltpu.VMEM((1, 2 * shards), F32),
            pltpu.VMEM((shards, 1, 2 * shards), F32),
            pltpu.VMEM((REP, 1, 2 * shards), F32),
            pltpu.VMEM((2, order, order), F32),
            pltpu.VMEM((2, order, order), F32),
            pltpu.VMEM((2, order, order), F32),
            pltpu.VMEM((2, order, order), BF16),
            pltpu.VMEM((2, order, order), BF16),
            pltpu.VMEM((2, order, order), BF16),
            pltpu.VMEM((2, order, order), BF16),
            pltpu.VMEM(row_shape[1:], BF16),
            dma((11,)),
            dma((6,)),
            dma((6,)),
            dma((2 * (REP - 1),)),
            dma((2 * (REP - 1),)),
            dma,
            dma((GROUPS,)),
            dma,
            dma((GROUPS,)),
            dma,
            dma((GROUPS,)),
            dma((GROUPS, 6)),
            dma((GROUPS, 6)),
            dma((GROUPS, 4)),
            dma((GROUPS, 4)),
            dma((2, 4)),
            dma((2, 4)),
            dma((2, 6)),
        ],
        compiler_params=pltpu.CompilerParams(
            collective_id=0, has_side_effects=True, vmem_limit_bytes=30 * 1024 * 1024
        ),
        name="shampoo_step",
    )(
        *(
            pltpu.with_memory_space_constraint(array, pltpu.HBM)
            for array in (block_slot.reshape(1, -1), grads, accum, vocab, left, right)
        )
    )


def finish_kernel(
    slot_ref,
    slots_ref,
    grad_ref,
    vocab_ref,
    rows_ref,
    accum_ref,
    left_ref,
    right_ref,
    vocab_accum_ref,
    direction_out,
    accum_out,
    left_out,
    right_out,
    vocab_out,
    step_out,
    direction,
    accum,
    stats,
    vocab_accum,
    vocab_step,
    sems,
):
    half = rows_ref.shape[-1]
    stores = []

    def store(source, target):
        stores.append(pltpu.make_async_copy(source, target, sems.at[len(stores)]))
        stores[-1].start()

    for slot in range(2):
        grad = gradient(slots_ref, slot)
        for side, (ref, out) in enumerate(((left_ref, left_out), (right_ref, right_out))):
            stats[side, slot] = ref[slot] + outer(grad, side)
            store(stats.at[side, slot], out.at[slot])
    for index in range(REP):
        quarter = grad_ref.shape[-1]
        columns = slice(index * quarter, (index + 1) * quarter)
        grad = grad_ref[index].astype(F32)
        accum[:, :, columns] = accum_ref[:, :, columns] + grad * grad
    store(accum, accum_out)
    for index in range(REP):
        quarter = vocab_ref.shape[-1]
        columns = slice(index * quarter, (index + 1) * quarter)
        vocab = vocab_ref[index].astype(F32)
        value = vocab_accum_ref[:, :, columns] + vocab * vocab
        vocab_accum[:, :, columns] = value
        vocab_step[:, :, columns] = (vocab / (jnp.sqrt(value) + 1e-10)).astype(BF16)
    store(vocab_accum, vocab_out)
    store(vocab_step, step_out)

    @pl.loop(0, direction.shape[0], unroll=4)
    def _(block):
        slot = slot_ref[block]
        owner, pick = slot // 2, lax.rem(slot, 2)
        for side in range(2):
            direction[block, :, side * half : (side + 1) * half] = rows_ref[2 * pick + side, owner]

    store(direction, direction_out)
    for copy in stores:
        copy.wait()


def finish(block_slot, slots, grads, vocab, rows, accum, left, right, vocab_accum):
    direction = (block_slot.shape[0], rows.shape[2], 2 * rows.shape[3])
    return pl.pallas_call(
        finish_kernel,
        out_shape=(
            jax.ShapeDtypeStruct(direction, BF16),
            jax.ShapeDtypeStruct(accum.shape, F32),
            jax.ShapeDtypeStruct(left.shape, F32),
            jax.ShapeDtypeStruct(right.shape, F32),
            jax.ShapeDtypeStruct(vocab_accum.shape, F32),
            jax.ShapeDtypeStruct(vocab_accum.shape, BF16),
        ),
        in_specs=[SMEM] + [VMEM] * 8,
        out_specs=(HBM,) * 6,
        scratch_shapes=[
            pltpu.VMEM(direction, BF16),
            pltpu.VMEM(accum.shape, F32),
            pltpu.VMEM((2,) + left.shape, F32),
            pltpu.VMEM(vocab_accum.shape, F32),
            pltpu.VMEM(vocab_accum.shape, BF16),
            pltpu.SemaphoreType.DMA((8,)),
        ],
        compiler_params=pltpu.CompilerParams(vmem_limit_bytes=30 * 1024 * 1024),
        name="finish",
    )(block_slot, slots, grads, vocab, rows, accum, left, right, vocab_accum)


def on_device(
    grad_blocks, graft_accum, left_stats, right_stats, block_slot, vocab_grads, vocab_accum
):
    slots, grads, vocab, rows = shampoo_step(
        block_slot, grad_blocks[0], graft_accum, vocab_grads[0], left_stats, right_stats
    )
    return finish(
        block_slot, slots, grads, vocab, rows, graft_accum, left_stats, right_stats, vocab_accum
    )


def solution(mesh):
    in_specs = (
        P("rep", None, "fsdp", None),
        P(None, "fsdp", None),
        P("fsdp", None, None),
        P("fsdp", None, None),
        P(),
        P("rep", None, "fsdp", None),
        P(None, "fsdp", None),
    )
    out_specs = (
        P(None, "fsdp", None),
        P(None, "fsdp", None),
        P("fsdp", None, None),
        P("fsdp", None, None),
        P(None, "fsdp", None),
        P(None, "fsdp", None),
    )
    return jax.shard_map(
        on_device, mesh=mesh, in_specs=in_specs, out_specs=out_specs, check_vma=False
    )
```

```python
import functools

import jax
import jax.numpy as jnp
from jax import lax
from jax.experimental import pallas as pl
from jax.experimental.pallas import tpu as pltpu
from jax.sharding import PartitionSpec as P

ITERS = 6
REP = 4
GROUPS = 2
TURNS = (0, 1)
MESH = pl.DeviceIdType.MESH
F32 = jnp.float32
BF16 = jnp.bfloat16
ANY = pl.BlockSpec(memory_space=pl.ANY)
HBM = pl.BlockSpec(memory_space=pltpu.HBM)
VMEM = pl.BlockSpec(memory_space=pltpu.VMEM)
SMEM = pl.BlockSpec(memory_space=pltpu.SMEM)


def remote(src, dst, send_sem, recv_sem, device):
    return pltpu.make_async_remote_copy(
        src_ref=src,
        dst_ref=dst,
        send_sem=send_sem,
        recv_sem=recv_sem,
        device_id=device,
        device_id_type=MESH,
    )


def enter(rep, own, shards):
    barrier = pltpu.get_barrier_semaphore()

    size = shards // GROUPS
    for turn in reversed(TURNS):
        group = lax.rem(own // size + turn, GROUPS)

        @pl.loop(1 if turn == 0 else 0, size)
        def _(step):
            other = group * size + lax.rem(own + step, size)
            pl.semaphore_signal(barrier, inc=1, device_id=(rep, other), device_id_type=MESH)

    for step in range(1, REP):
        other = lax.rem(rep + step, REP)
        pl.semaphore_signal(barrier, inc=1, device_id=(other, own), device_id_type=MESH)
    return lambda: pl.semaphore_wait(barrier, shards - 1 + REP - 1)


class RingGather:
    def __init__(self, out, first, count, rep, own, send_sems, recv_sems):
        self.send_sems, self.recv_sems = send_sems, recv_sems
        right, left = lax.rem(rep + 1, REP), lax.rem(rep + REP - 1, REP)
        far = lax.rem(rep + 2, REP)
        half = count // 2
        whole, front, back = pl.ds(first, count), pl.ds(first, half), pl.ds(first + half, half)
        to_right, to_left = (right, own), (left, own)
        self.sends = (
            self.copy(out.at[rep, whole], 0, to_right),
            self.copy(out.at[rep, whole], 1, to_left),
            self.copy(out.at[left, front], 2, to_right),
            self.copy(out.at[right, back], 3, to_left),
        )
        self.arrivals = (
            self.copy(out.at[left, whole], 0, to_right),
            self.copy(out.at[right, whole], 1, to_left),
            self.copy(out.at[far, front], 2, to_right),
            self.copy(out.at[far, back], 3, to_left),
        )

    def copy(self, piece, index, device):
        return remote(piece, piece, self.send_sems.at[index], self.recv_sems.at[index], device)

    def start(self):
        self.sends[0].start()
        self.sends[1].start()

    def forward(self):
        self.arrivals[0].wait_recv()
        self.sends[2].start()
        self.arrivals[1].wait_recv()
        self.sends[3].start()

    def finish(self):
        self.arrivals[2].wait_recv()
        self.arrivals[3].wait_recv()

    def sent(self):
        for send in self.sends:
            send.wait_send()


class PairGather:
    def __init__(self, slots, first, count, rep, own, send_sems, recv_sems):
        self.send_sems, self.recv_sems = send_sems, recv_sems
        odd = lax.rem(rep, 2)
        partner, beside = rep + 1 - 2 * odd, lax.rem(rep + 3 + 2 * odd, REP)
        far = lax.rem(rep + 2, REP)
        pick, rows = rep // 2, pl.ds(first, count)
        other = 1 - pick
        to_partner, to_beside = (partner, own), (beside, own)

        def copy(slot, index, sem, device):
            piece = slots.at[slot, index, rows]
            return remote(piece, piece, send_sems.at[sem], recv_sems.at[sem], device)

        self.sends = (
            copy(pick, rep, 0, to_partner),
            copy(other, rep, 1, to_beside),
            copy(pick, beside, 2, to_partner),
        )
        self.arrivals = (
            copy(pick, partner, 0, to_partner),
            copy(pick, beside, 1, to_beside),
            copy(pick, far, 2, to_partner),
        )
        self.rest = (
            copy(other, rep, 3, to_partner),
            copy(pick, rep, 4, to_beside),
            copy(pick, partner, 5, to_beside),
        )
        self.rest_arrivals = (
            copy(other, partner, 3, to_partner),
            copy(other, beside, 4, to_beside),
            copy(other, far, 5, to_beside),
        )

    def start(self):
        self.sends[0].start()
        self.sends[1].start()

    def forward(self):
        self.arrivals[1].wait_recv()
        self.sends[2].start()

    def finish(self):
        self.arrivals[0].wait_recv()
        self.arrivals[2].wait_recv()

    def sent(self):
        for send in self.sends:
            send.wait_send()

    def start_rest(self):
        for send in self.rest:
            send.start()

    def finish_rest(self):
        for arrival in self.rest_arrivals:
            arrival.wait_recv()
        for send in self.rest:
            send.wait_send()


class Exchange:
    def __init__(self, shards, rep, own, source, target, span, send_sem, recv_sems):
        self.shards, self.rep, self.own = shards, rep, own
        self.source, self.target, self.span = source, target, span
        self.send_sem, self.recv_sems = send_sem, recv_sems
        self.size = shards // GROUPS

    def start(self):
        size = self.size
        for turn in TURNS:
            group = lax.rem(self.own // size + turn, GROUPS)

            def send(step):
                other = group * size + lax.rem(self.own + step, size)
                remote(
                    self.source(other),
                    self.target(self.own),
                    self.send_sem,
                    self.recv_sems.at[turn],
                    (self.rep, other),
                ).start()

            @pl.loop(0, size // 2 - 1)
            def _(away):
                send(size // 2 + away)
                send(size // 2 - 1 - away)

            send(size - 1)
            if turn:
                send(0)

    def whole(self, first, count, turn):
        span = self.span(first, count)
        return remote(span, span, self.send_sem, self.recv_sems.at[turn], (self.rep, self.own))

    def arrive(self, turn):
        first = lax.rem(self.own // self.size + GROUPS - turn, GROUPS) * self.size
        self.whole(first, self.size if turn else self.size - 1, turn).wait_recv()
        return first

    def finish(self):
        self.whole(0, self.shards - 1, 0).wait_send()


def gather_groups(ring_type, exchange, out, kept, ring_sends, ring_recvs):
    rings = []
    for index, turn in enumerate(TURNS):
        first = exchange.arrive(turn)
        if turn == 0:
            kept.wait()
        ring = ring_type(
            out, first, exchange.size, exchange.rep, exchange.own, ring_sends.at[index], ring_recvs.at[index]
        )
        ring.start()
        if rings:
            rings[-1].forward()
        rings.append(ring)
    rings[-1].forward()
    for ring in rings:
        ring.finish()

    def sent():
        exchange.finish()
        for ring in rings:
            ring.sent()

    return sent


def product(left, right):
    return jnp.dot(left, right, preferred_element_type=F32)


def symmetric_product(left, right, side):
    half = left.shape[-1] // 2
    return product(left[side, :half], right[side, :, :half]), product(left[side], right[side, :, half:])


def parts_of(matrix, side):
    half = matrix.shape[-1] // 2
    return matrix[side, :half, :half], matrix[side, :, half:]


def put_parts(matrix, side, parts):
    half = matrix.shape[-1] // 2
    matrix[side, :half, :half] = parts[0]
    matrix[side, :, half:] = parts[1]


def put_operand(matrix, side, parts):
    half = matrix.shape[-1] // 2
    corner, right = (part.astype(BF16) for part in parts)
    put_parts(matrix, side, (corner, right))
    matrix[side, half:, :half] = right[:half].T


def combine(parts, factor, others, other_factor):
    return tuple(part * factor + other * other_factor for part, other in zip(parts, others))


def gradient(slots_ref, slot):
    count, shards, rows, quarter = slots_ref.shape[1:]
    return jnp.concatenate(
        [
            slots_ref[slot, index].astype(F32).reshape(shards * rows, quarter).astype(BF16)
            for index in range(count)
        ],
        axis=1,
    )


def outer(grad, side):
    axis = 1 - side
    return lax.dot_general(grad, grad, (((axis,), (axis,)), ((), ())), preferred_element_type=F32)


def step_kernel(
    shards,
    slot_ref,
    grad_ref,
    accum_ref,
    vocab_ref,
    left_ref,
    right_ref,
    vocab_accum_ref,
    accum_out,
    left_out,
    right_out,
    vocab_out,
    step_out,
    rows_out,
    grad_all,
    vocab_all,
    accum_all,
    vocab_accum,
    vocab_step,
    slot_own,
    grad_own,
    grad_terms,
    grad_relay,
    grad_sum,
    accum_own,
    vocab_own,
    vocab_terms,
    vocab_sum,
    placement,
    outgoing,
    slots,
    graft_part,
    graft_parts,
    graft_totals,
    stats,
    scaled,
    result,
    scaled_operand,
    excess_operand,
    change_operand,
    result_operand,
    mine,
    local_sems,
    grad_sends,
    grad_recvs,
    term_sends,
    term_recvs,
    slot_sends,
    slot_recvs,
    part_sends,
    part_recvs,
    row_sends,
    row_recvs,
    slot_ring_sends,
    slot_ring_recvs,
    row_ring_sends,
    row_ring_recvs,
    sum_ring_sends,
    sum_ring_recvs,
    slot_rest_sems,
    store_sems,
):
    rep, own = lax.axis_index("rep"), lax.axis_index("fsdp")
    right, left, far = (lax.rem(rep + step, REP) for step in (1, REP - 1, 2))
    to_right, to_left = (right, own), (left, own)
    pick, half = rep // 2, lax.rem(rep, 2)
    blocks, rows, quarter = grad_own.shape
    vocab_quarter = vocab_own.shape[-1]
    order = stats.shape[-1]

    def grad_columns(index):
        return pl.ds(pl.multiple_of(index * quarter, 128), quarter)

    def vocab_columns(index):
        return pl.ds(pl.multiple_of(index * vocab_quarter, 128), vocab_quarter)

    loads = (
        pltpu.make_async_copy(grad_ref.at[:, :, grad_columns(rep)], grad_own, local_sems.at[0]),
        pltpu.make_async_copy(accum_ref.at[:, :, grad_columns(rep)], accum_own, local_sems.at[1]),
        pltpu.make_async_copy(vocab_ref.at[:, :, vocab_columns(rep)], vocab_own, local_sems.at[2]),
        pltpu.make_async_copy(left_ref, stats.at[0], local_sems.at[3]),
        pltpu.make_async_copy(right_ref, stats.at[1], local_sems.at[4]),
        pltpu.make_async_copy(accum_ref, accum_all, local_sems.at[7]),
        pltpu.make_async_copy(vocab_accum_ref, vocab_accum, local_sems.at[11]),
    )
    load_slot = pltpu.make_async_copy(slot_ref, slot_own, local_sems.at[10])
    load_slot.start()
    entered = enter(rep, own, shards)
    for load in loads:
        load.start()

    total_rows = blocks * rows
    spread = jnp.where(
        lax.broadcasted_iota(jnp.int32, (blocks, total_rows), 0)
        == lax.broadcasted_iota(jnp.int32, (blocks, total_rows), 1) // rows,
        1.0,
        0.0,
    )
    load_slot.wait()
    slot_of = jnp.broadcast_to(slot_own[...], (8, blocks)).astype(F32)
    slot_of = product(slot_of.astype(BF16), spread.astype(BF16))[:1].astype(jnp.int32)
    key = slot_of * rows + lax.rem(lax.broadcasted_iota(jnp.int32, (1, total_rows), 1), rows)
    key = jnp.broadcast_to(key, (shards * rows, total_rows))
    row = lax.broadcasted_iota(jnp.int32, (shards * rows, total_rows), 0)
    place = (row // rows) * (2 * rows) + lax.rem(row, rows)
    for slot in range(2):
        placement[slot] = jnp.where(key == place + slot * rows, 1.0, 0.0).astype(BF16)

    entered()
    front, back = pl.ds(0, blocks // 2), pl.ds(blocks // 2, blocks // 2)
    grad_pairs = (
        (grad_ref.at[front, :, grad_columns(far)], grad_relay.at[0], to_right),
        (grad_ref.at[back, :, grad_columns(far)], grad_relay.at[1], to_left),
        (grad_ref.at[:, :, grad_columns(right)], grad_terms.at[0], to_right),
        (grad_ref.at[:, :, grad_columns(left)], grad_terms.at[1], to_left),
        (grad_relay.at[0], grad_terms.at[2, front], to_right),
        (grad_relay.at[1], grad_terms.at[2, back], to_left),
    )
    grad_copies = [
        remote(source, target, grad_sends.at[index], grad_recvs.at[index], device)
        for index, (source, target, device) in enumerate(grad_pairs)
    ]
    for copy in grad_copies[:4]:
        copy.start()
    vocab_copies = []
    for step in range(1, REP):
        other = lax.rem(rep + step, REP)
        vocab_copies.append(
            remote(
                vocab_ref.at[:, :, vocab_columns(other)],
                vocab_terms.at[step - 1],
                term_sends.at[step - 1],
                term_recvs.at[step - 1],
                (other, own),
            )
        )
    for index in range(2):
        grad_copies[index].wait_recv()
        grad_copies[4 + index].start()
    loads[0].wait()
    for copy in grad_copies[2:]:
        copy.wait_recv()
    total = grad_own[...].astype(F32)
    for step in range(REP - 1):
        total = total + grad_terms[step].astype(F32)
    flat = total.reshape(total_rows, quarter).astype(BF16)
    for slot in range(2):
        placed = jnp.dot(placement[slot], flat, preferred_element_type=F32)
        outgoing[:, slot] = placed.reshape(shards, rows, quarter).astype(BF16)
    slot_exchange = Exchange(
        shards,
        rep,
        own,
        lambda other: outgoing.at[other],
        lambda source: slots.at[:, rep, source],
        lambda first, count: slots.at[:, rep, pl.ds(first, count)],
        slot_sends,
        slot_recvs,
    )
    slot_exchange.start()
    keep = pltpu.make_async_copy(outgoing.at[own], slots.at[:, rep, own], local_sems.at[5])
    keep.start()
    for copy in vocab_copies:
        copy.start()
    grad_sum[...] = total.astype(BF16)
    keep_sum = pltpu.make_async_copy(grad_sum, grad_all.at[rep], local_sems.at[6])
    keep_sum.start()

    loads[1].wait()
    value = flat.astype(F32)
    accum_new = accum_own[...].reshape(total_rows, quarter) + value * value
    grafted = value / (jnp.sqrt(accum_new) + 1e-10)
    slot_count = 2 * shards
    slot = lax.broadcasted_iota(jnp.int32, (slot_count, total_rows), 0)
    chosen = jnp.where(jnp.broadcast_to(slot_of, (slot_count, total_rows)) == slot, 1.0, 0.0)
    by_slot = jnp.dot(chosen, grafted * grafted, precision=lax.Precision.HIGHEST)
    ones = jnp.ones((8, quarter), F32)
    parts = lax.dot_general(
        ones, by_slot, (((1,), (1,)), ((), ())), precision=lax.Precision.HIGHEST
    )
    graft_part[...] = parts[:1]
    graft_parts[pl.ds(own, 1)] = parts[:1][None]
    part_exchange = Exchange(
        shards,
        rep,
        own,
        lambda other: graft_part,
        lambda source: graft_parts.at[source],
        lambda first, count: graft_parts.at[pl.ds(first, count)],
        part_sends,
        part_recvs,
    )
    part_exchange.start()

    slots_sent = gather_groups(PairGather, slot_exchange, slots, keep, slot_ring_sends, slot_ring_recvs)
    slot_rest = PairGather(slots, 0, shards, rep, own, slot_rest_sems.at[0], slot_rest_sems.at[1])
    slot_rest.start_rest()
    keep_sum.wait()
    grad_ring = RingGather(grad_all, 0, blocks, rep, own, sum_ring_sends.at[0], sum_ring_recvs.at[0])
    grad_ring.start()
    keep_vocab = pltpu.make_async_copy(vocab_sum, vocab_all.at[rep], local_sems.at[8])
    vocab_ring = RingGather(
        vocab_all, 0, vocab_own.shape[0], rep, own, sum_ring_sends.at[1], sum_ring_recvs.at[1]
    )
    total_copies = []
    for step in range(1, REP):
        other, source = lax.rem(rep + step, REP), lax.rem(rep + REP - step, REP)
        index = REP - 1 + step - 1
        pieces = [graft_totals.at[pl.ds(place, 1)] for place in (rep, source)]
        total_copies.append(
            [remote(piece, piece, term_sends.at[index], term_recvs.at[index], (other, own)) for piece in pieces]
        )

    grad = gradient(slots, pick)
    middle = order // 2
    row = lax.broadcasted_iota(jnp.int32, (order, order), 0)
    column = lax.broadcasted_iota(jnp.int32, (order, order), 1)
    identity = jnp.where(row == column, 1.25, 0.0)
    identity = (identity[:middle, :middle], identity[:, middle:])
    starts = []
    for side in range(2):
        loads[3 + side].wait()
        start = []
        for part, lines, columns in zip(
            (stats[side, pick, :middle, :middle], stats[side, pick, :, middle:]), (slice(0, middle), slice(None)), (slice(0, middle), slice(middle, None))
        ):
            if side == 0:
                pair, dims = (grad[lines], grad[columns]), (((1,), (1,)), ((), ()))
            else:
                pair, dims = (grad[:, lines], grad[:, columns]), (((0,), (0,)), ((), ()))
            start.append(part + lax.dot_general(*pair, dims, preferred_element_type=F32))
        starts.append(start)
    for side in range(2):
        corner, right_half = starts[side]
        squares = jnp.sum(corner * corner) + jnp.sum(right_half * right_half)
        squares = squares + jnp.sum(right_half[:middle] * right_half[:middle])
        inverse = 1.0 / jnp.sqrt(jnp.full((1, 1), squares, F32))
        value = (corner * inverse, right_half * inverse)
        put_parts(scaled, side, value)
        put_operand(scaled_operand, side, value)
        root = combine(identity, 1.0, value, -0.25)
        put_parts(result, side, root)
        put_operand(result_operand, side, root)

    @pl.loop(1, ITERS)
    def _(iteration):
        excess = []
        for side in range(2):
            square = symmetric_product(scaled_operand, scaled_operand, side)
            excess.append(combine(square, 0.0625, parts_of(scaled, side), -0.625))
            put_operand(excess_operand, side, excess[side])
        for side in range(2):
            change = symmetric_product(excess_operand, excess_operand, side)
            put_operand(change_operand, side, combine(change, 1.0, excess[side], 3.125))
        for side in range(2):
            value = symmetric_product(change_operand, scaled_operand, side)
            value = combine(value, 1.0, parts_of(scaled, side), 2.44140625)
            put_parts(scaled, side, value)
            put_operand(scaled_operand, side, value)
        for side in range(2):
            root = symmetric_product(result_operand, scaled_operand, side)
            root = combine(root, -0.25, parts_of(result, side), 1.25)
            put_parts(result, side, root)
            put_operand(result_operand, side, root)

        @pl.when(iteration == 3)
        def _():
            for turn in TURNS:
                part_exchange.arrive(turn)
            graft_totals[pl.ds(rep, 1)] = jnp.sum(graft_parts[...], axis=0)[None]
            for copy, arrival in total_copies:
                copy.start()
            loads[2].wait()
            for copy in vocab_copies:
                copy.wait_recv()
            vocab_total = vocab_own[...].astype(F32)
            for step in range(REP - 1):
                vocab_total = vocab_total + vocab_terms[step].astype(F32)
            vocab_sum[...] = vocab_total.astype(BF16)
            keep_vocab.start()

        @pl.when(iteration == 4)
        def _():
            keep_vocab.wait()
            vocab_ring.start()

    shampoo = product(product(result_operand[0], grad).astype(BF16), result_operand[1])
    for copy, arrival in total_copies:
        arrival.wait_recv()
    entries = float(order * order)
    lane = lax.broadcasted_iota(jnp.int32, (1, slot_count), 1)
    graft_total = jnp.sum(jnp.where(lane == 2 * own + pick, jnp.sum(graft_totals[...], axis=0), 0.0))
    graft_mean = jnp.full((1, 1), graft_total / entries, F32)
    shampoo_mean = jnp.full((1, 1), jnp.sum(shampoo * shampoo) / entries, F32)
    scale = jnp.sqrt(graft_mean) / jnp.sqrt(shampoo_mean + 1e-06)
    direction = shampoo * scale
    direction = jnp.where(half == 0, direction[:, : order // 2], direction[:, order // 2 :])
    mine[...] = direction.reshape(mine.shape).astype(BF16)
    row_exchange = Exchange(
        shards,
        rep,
        own,
        lambda other: mine.at[other],
        lambda source: rows_out.at[rep, source],
        lambda first, count: rows_out.at[rep, pl.ds(first, count)],
        row_sends,
        row_recvs,
    )
    row_exchange.start()
    keep_rows = pltpu.make_async_copy(mine.at[own], rows_out.at[rep, own], local_sems.at[9])
    keep_rows.start()
    grad_ring.forward()
    vocab_ring.forward()
    slot_rest.finish_rest()

    stores = []

    def store(source, target):
        stores.append(pltpu.make_async_copy(source, target, store_sems.at[len(stores)]))
        stores[-1].start()

    for slot in range(2):
        grad = gradient(slots, slot)
        for side, out in enumerate((left_out, right_out)):
            stats[side, slot] = stats[side, slot] + outer(grad, side)
            store(stats.at[side, slot], out.at[slot])
    loads[5].wait()
    loads[6].wait()
    grad_ring.finish()
    vocab_ring.finish()
    for index in range(REP):
        columns = slice(index * quarter, (index + 1) * quarter)
        grad = grad_all[index].astype(F32)
        accum_all[:, :, columns] = accum_all[:, :, columns] + grad * grad
        columns = slice(index * vocab_quarter, (index + 1) * vocab_quarter)
        vocab = vocab_all[index].astype(F32)
        value = vocab_accum[:, :, columns] + vocab * vocab
        vocab_accum[:, :, columns] = value
        vocab_step[:, :, columns] = (vocab / (jnp.sqrt(value) + 1e-10)).astype(BF16)
    store(accum_all, accum_out)
    store(vocab_accum, vocab_out)
    store(vocab_step, step_out)
    rows_sent = gather_groups(RingGather, row_exchange, rows_out, keep_rows, row_ring_sends, row_ring_recvs)

    for copy in stores:
        copy.wait()
    for copy in grad_copies + vocab_copies:
        copy.wait_send()
    for copy, arrival in total_copies:
        copy.wait_send()
    part_exchange.finish()
    grad_ring.sent()
    vocab_ring.sent()
    slots_sent()
    rows_sent()


def shampoo_step(block_slot, grads, accum, vocab, left, right, vocab_accum):
    shards = lax.axis_size("fsdp")
    blocks, rows, order = grads.shape
    quarter = order // REP
    vocab_shape = vocab.shape[:2] + (vocab.shape[-1] // REP,)
    row_shape = (REP, shards, rows, order // 2)
    slot_shape = (2, REP, shards, rows, quarter)
    dma = pltpu.SemaphoreType.DMA
    return pl.pallas_call(
        functools.partial(step_kernel, shards),
        out_shape=(
            jax.ShapeDtypeStruct(accum.shape, F32),
            jax.ShapeDtypeStruct(left.shape, F32),
            jax.ShapeDtypeStruct(right.shape, F32),
            jax.ShapeDtypeStruct(vocab_accum.shape, F32),
            jax.ShapeDtypeStruct(vocab_accum.shape, BF16),
            jax.ShapeDtypeStruct(row_shape, BF16),
        ),
        in_specs=[HBM] * 7,
        out_specs=(ANY,) * 6,
        scratch_shapes=[
            pltpu.VMEM((REP, blocks, rows, quarter), BF16),
            pltpu.VMEM((REP,) + vocab_shape, BF16),
            pltpu.VMEM(accum.shape, F32),
            pltpu.VMEM(vocab_accum.shape, F32),
            pltpu.VMEM(vocab_accum.shape, BF16),
            pltpu.VMEM((1, blocks), jnp.int32),
            pltpu.VMEM((blocks, rows, quarter), BF16),
            pltpu.VMEM((REP - 1, blocks, rows, quarter), BF16),
            pltpu.VMEM((2, blocks // 2, rows, quarter), BF16),
            pltpu.VMEM((blocks, rows, quarter), BF16),
            pltpu.VMEM((blocks, rows, quarter), F32),
            pltpu.VMEM(vocab_shape, BF16),
            pltpu.VMEM((REP - 1,) + vocab_shape, BF16),
            pltpu.VMEM(vocab_shape, BF16),
            pltpu.VMEM((2, shards * rows, blocks * rows), BF16),
            pltpu.VMEM((shards, 2, rows, quarter), BF16),
            pltpu.VMEM(slot_shape, BF16),
            pltpu.VMEM((1, 2 * shards), F32),
            pltpu.VMEM((shards, 1, 2 * shards), F32),
            pltpu.VMEM((REP, 1, 2 * shards), F32),
            pltpu.VMEM((2, 2, order, order), F32),
            pltpu.VMEM((2, order, order), F32),
            pltpu.VMEM((2, order, order), F32),
            pltpu.VMEM((2, order, order), BF16),
            pltpu.VMEM((2, order, order), BF16),
            pltpu.VMEM((2, order, order), BF16),
            pltpu.VMEM((2, order, order), BF16),
            pltpu.VMEM(row_shape[1:], BF16),
            dma((12,)),
            dma((6,)),
            dma((6,)),
            dma((2 * (REP - 1),)),
            dma((2 * (REP - 1),)),
            dma,
            dma((GROUPS,)),
            dma,
            dma((GROUPS,)),
            dma,
            dma((GROUPS,)),
            dma((GROUPS, 6)),
            dma((GROUPS, 6)),
            dma((GROUPS, 4)),
            dma((GROUPS, 4)),
            dma((2, 4)),
            dma((2, 4)),
            dma((2, 6)),
            dma((7,)),
        ],
        compiler_params=pltpu.CompilerParams(
            collective_id=0, has_side_effects=True, vmem_limit_bytes=30 * 1024 * 1024
        ),
        name="shampoo_step",
    )(
        *(
            pltpu.with_memory_space_constraint(array, pltpu.HBM)
            for array in (block_slot.reshape(1, -1), grads, accum, vocab, left, right, vocab_accum)
        )
    )


def finish_kernel(slot_ref, rows_ref, *refs):
    count = (len(refs) - 2) // 2
    sources, (direction_out, *targets), (direction, sems) = refs[:count], refs[count:-2], refs[-2:]
    stores = [
        pltpu.make_async_copy(source, target, sems.at[index])
        for index, (source, target) in enumerate(zip(sources, targets))
    ]
    for copy in stores:
        copy.start()
    half = rows_ref.shape[-1]

    @pl.loop(0, direction.shape[0], unroll=4)
    def _(block):
        slot = slot_ref[block]
        owner, pick = slot // 2, lax.rem(slot, 2)
        for side in range(2):
            direction[block, :, side * half : (side + 1) * half] = rows_ref[2 * pick + side, owner]

    stores.append(pltpu.make_async_copy(direction, direction_out, sems.at[count]))
    stores[-1].start()
    for copy in stores:
        copy.wait()


def finish(block_slot, rows, *others):
    direction = (block_slot.shape[0], rows.shape[2], 2 * rows.shape[3])
    return pl.pallas_call(
        finish_kernel,
        out_shape=(jax.ShapeDtypeStruct(direction, BF16),)
        + tuple(jax.ShapeDtypeStruct(other.shape, other.dtype) for other in others),
        in_specs=[SMEM, VMEM] + [ANY] * len(others),
        out_specs=(HBM,) * (1 + len(others)),
        scratch_shapes=[pltpu.VMEM(direction, BF16), pltpu.SemaphoreType.DMA((1 + len(others),))],
        compiler_params=pltpu.CompilerParams(vmem_limit_bytes=8 * 1024 * 1024),
        name="finish",
    )(block_slot, rows, *others)


def on_device(
    grad_blocks, graft_accum, left_stats, right_stats, block_slot, vocab_grads, vocab_accum
):
    *others, rows = shampoo_step(
        block_slot, grad_blocks[0], graft_accum, vocab_grads[0], left_stats, right_stats, vocab_accum
    )
    return tuple(finish(block_slot, rows, *others))


def solution(mesh):
    in_specs = (
        P("rep", None, "fsdp", None),
        P(None, "fsdp", None),
        P("fsdp", None, None),
        P("fsdp", None, None),
        P(),
        P("rep", None, "fsdp", None),
        P(None, "fsdp", None),
    )
    out_specs = (
        P(None, "fsdp", None),
        P(None, "fsdp", None),
        P("fsdp", None, None),
        P("fsdp", None, None),
        P(None, "fsdp", None),
        P(None, "fsdp", None),
    )
    return jax.shard_map(
        on_device, mesh=mesh, in_specs=in_specs, out_specs=out_specs, check_vma=False
    )
```
